512 devices in a mesh: lag: 64 (over z, y), par: 8 (over x, core).
Axes of the slice: x: 4, y: 4, z: 16, core: 2. Of those that a mesh axis runs over, the one named last changes fastest.
Arguments:
- prior_rows: bfloat16 [64, 512, 16384], P('lag', None, 'par'), may hold values from -0.0625 to 0.0625
- raw_rows: bfloat16 [64, 512, 16384], P('lag', None, 'par'), may hold values from -6 to 6
Outputs:
- diag_zero: float32 [64, 512, 512], P('lag', 'par')
- diag_one: float32 [64, 512, 512], P('lag', 'par')
The draws below stay inside these ranges and needn't reach their ends.
All inputs are finite; a program needn't handle non-finite values.
Results may differ from the reference program's by a relative error of at most 0.0003.
Values may be sent and summed in bfloat16 or wider, within the bound.
No kernel may reach another device: no remote copies, remote signals or barrier semaphores. Data moves between devices by JAX's collectives and lax.ppermute only.
A program may use at most 64 MiB of HBM per device.

```python
import jax
import jax.numpy as jnp
from jax import lax

SENSORS = 512
LAGS = 64
PANEL = 16384


def with_spikes(result, key, source, target, shards_of, factor):
    owner, partner = [(jnp.arange(result.shape[position]) // (result.shape[position] // shards_of)).reshape([-1 if axis == position else 1 for axis in range(result.ndim)]) for position in (source, target)]
    chosen = jax.random.permutation(key, shards_of)[partner]
    strong = (owner == chosen) | (owner == (partner + shards_of // 2) % shards_of)
    return jnp.where(strong, factor * result, result)


def block_scale(key, extent, shards, smallest, top_value):
    def one(position, parts):
        heights = jax.random.uniform(jax.random.fold_in(jax.random.fold_in(key, 6), position), (parts,), jnp.float32, smallest / len(shards), top_value / len(shards))
        return jnp.repeat(jnp.exp(heights), extent[position] // parts).reshape((-1,) + (1,) * (len(extent) - position - 1))

    loudness = one(*shards[0])
    for cut in shards[1:]:
        loudness = loudness * one(*cut)
    return loudness


def normal_values(rng, extent, scale, limit, pieces=(), kind=jnp.bfloat16):
    array = scale * jax.random.normal(rng, extent, jnp.float32)
    if pieces:
        array = array * block_scale(rng, extent, pieces, -0.22, 0.18)
    return jnp.clip(array, -limit, limit).astype(kind)


def bell_draw_with(own_key, dims, spread, bound, pieces, heavy, kind=jnp.bfloat16):
    result = spread * jax.random.normal(own_key, dims, jnp.float32)
    if pieces:
        result = result * block_scale(own_key, dims, pieces, -0.22, 0.18)
    return jnp.clip(with_spikes(result, jax.random.fold_in(own_key, 3), *heavy), -bound, bound).astype(kind)


def setup_inputs(seed: int = 0) -> dict:
    arg_keys = jax.random.split(jax.random.key(seed), 3)
    return {
        "prior_rows": bell_draw_with(arg_keys[0], (LAGS, SENSORS, PANEL), PANEL ** -0.5, 0.0625, ((0, 64), (2, 8)), (2, 1, 8, 2.0)),
        "raw_rows": normal_values(arg_keys[1], (LAGS, SENSORS, PANEL), 1.0, 6.0, ((0, 64), (2, 8))),
    }


def lag_tiles(blocks):
    prior_block, raw_block, next_block = blocks
    tile_zero = jnp.dot(prior_block, raw_block.T, preferred_element_type=jnp.float32)
    tile_one = jnp.dot(prior_block, next_block.T, preferred_element_type=jnp.float32)
    return tile_zero, tile_one


def reference(prior_rows, raw_rows):
    following = jnp.concatenate([raw_rows[1:], jnp.zeros_like(raw_rows[:1])], axis=0)
    tile_zero, tile_one = lax.map(lag_tiles, (prior_rows, raw_rows, following))
    return jnp.cumsum(tile_zero, axis=0), jnp.cumsum(tile_one, axis=0)
```

```python
import jax
import jax.numpy as jnp
import numpy as np
from jax import lax
from jax.experimental import pallas as pl
from jax.experimental.pallas import tpu as pltpu
from jax.sharding import Mesh, PartitionSpec as P

F32 = jnp.float32
NT = (((1,), (1,)), ((), ()))
LAG = ("z", "y")
PAR = ("x", "core")
VMEM = pl.BlockSpec(memory_space=pltpu.VMEM)


def call(kernel, out_shape, *args):
    return pl.pallas_call(
        kernel,
        out_shape=out_shape,
        in_specs=[VMEM] * len(args),
        out_specs=jax.tree.map(lambda _: VMEM, out_shape),
    )(*args)


def shape(*dims):
    return jax.ShapeDtypeStruct(dims, F32)


def tile_zero_kernel(prior, raw, out):
    for x in range(4):
        part = lax.dot_general(prior[x * 128 : (x + 1) * 128], raw[...], NT, preferred_element_type=F32)
        for c in range(2):
            out[c, x] = part[c * 64 : (c + 1) * 64]


def tile_one_kernel(prior, raw_next, prior_last, raw, out):
    for x in range(4):
        rows = slice(x * 128, (x + 1) * 128)
        part = lax.dot_general(prior[rows], raw_next[...], NT, preferred_element_type=F32)
        part += lax.dot_general(prior_last[rows], raw[...], NT, preferred_element_type=F32)
        for c in range(2):
            for y in range(4):
                first = c * 64 + y * 16
                out[y, x, c] = part[first : first + 16]


def add_kernel(parts, out):
    total = parts[0]
    for i in range(1, parts.shape[0]):
        total = total + parts[i]
    out[...] = total


def spread(ref, half, value, first):
    for i in range(2):
        for j in range(4):
            tile = value[i * 8 : (i + 1) * 8, j * 128 : (j + 1) * 128]
            ref[first + i * 4 + j, half * 8 : (half + 1) * 8, :] = tile


def gathered(ref, half, first):
    rows = []
    for i in range(2):
        tiles = [ref[first + i * 4 + j, half * 8 : (half + 1) * 8, :] for j in range(4)]
        rows.append(jnp.concatenate(tiles, axis=1))
    return jnp.concatenate(rows, axis=0)


def local_prefix_kernel(zero, one, local, ahead):
    total_zero, total_one, delayed = None, None, []
    for lag in range(4):
        here, late = one[lag, 0, 0], one[lag, 0, 1]
        for x in range(1, 4):
            here, late = here + one[lag, x, 0], late + one[lag, x, 1]
        total_zero = zero[lag] if lag == 0 else total_zero + zero[lag]
        local[lag, 0] = total_zero
        if lag == 0:
            spread(ahead, 1, late, 8)
            total_one = here + late
        else:
            local[lag - 1, 1] = total_one + late
            total_one = total_one + here + late
    local[3, 1] = total_one
    spread(ahead, 0, total_zero, 0)
    spread(ahead, 0, total_one, 8)
    spread(ahead, 1, jnp.zeros_like(total_zero), 0)


def lag_scan_kernel(ahead, back):
    state = jnp.zeros((8, 128), F32)
    for z in range(16):
        back[z, 0:8] = state
        state = state + ahead[z, 0:8]
        back[z, 8:16] = ahead[z + 1, 8:16] if z < 15 else jnp.zeros((8, 128), F32)


def finish_kernel(local, back, out):
    earlier_zero, earlier_one, late = gathered(back, 0, 0), gathered(back, 0, 8), gathered(back, 1, 8)
    for lag in range(4):
        out[lag, 0:16] = local[lag, 0] + earlier_zero
        last = local[lag, 1] + earlier_one
        out[lag, 16:32] = last + late if lag == 3 else last


def split_kernel(rows, zero, one):
    for y in range(4):
        zero[0, y * 16 : (y + 1) * 16] = rows[y, 0:16]
        one[0, y * 16 : (y + 1) * 16] = rows[y, 16:32]


def exchange(value, axes):
    return lax.all_to_all(value, axes, 0, 0, tiled=True)


def body(prior_rows, raw_rows):
    prior, raw = prior_rows[0], raw_rows[0]
    device = np.arange(512).reshape(64, 4, 2)
    down = [(int(device[l + 1, x, 0]), int(device[l, x, 0])) for l in range(63) for x in range(4)]
    up = [(int(device[l, x, 1]), int(device[l + 1, x, 1])) for l in range(63) for x in range(4)]
    everyone = LAG + PAR
    raw_next = lax.ppermute(raw, everyone, down)
    prior_last = lax.ppermute(prior, everyone, up)

    zero = call(tile_zero_kernel, shape(2, 4, 64, 512), prior, raw)
    zero = call(add_kernel, shape(4, 64, 512), exchange(zero, "core"))
    zero = call(add_kernel, shape(64, 512), exchange(zero, "x"))
    zero = exchange(zero.reshape(4, 16, 512), "y")

    raw_next, prior_last, zero = lax.optimization_barrier((raw_next, prior_last, zero))
    one = call(tile_one_kernel, shape(4, 4, 2, 16, 512), prior, raw_next, prior_last, raw)
    one = exchange(one.reshape(32, 16, 512), ("y", "x", "core")).reshape(4, 4, 2, 16, 512)

    local, ahead = call(local_prefix_kernel, (shape(4, 2, 16, 512), shape(16, 16, 128)), zero, one)
    back = call(lag_scan_kernel, shape(16, 16, 128), exchange(ahead, "z"))
    rows = call(finish_kernel, shape(4, 32, 512), local, exchange(back, "z"))
    return tuple(call(split_kernel, (shape(1, 64, 512), shape(1, 64, 512)), exchange(rows, "y")))


def solution(mesh):
    chips = Mesh(mesh.devices.reshape(16, 4, 4, 2), LAG + PAR)
    in_specs = (P(LAG, None, PAR), P(LAG, None, PAR))
    out_specs = (P(LAG, PAR, None), P(LAG, PAR, None))
    return jax.shard_map(body, mesh=chips, in_specs=in_specs, out_specs=out_specs, check_vma=False)
```

```python
import jax
import jax.numpy as jnp
import numpy as np
from jax import lax
from jax.experimental import pallas as pl
from jax.experimental.pallas import tpu as pltpu
from jax.sharding import Mesh, PartitionSpec as P

F32 = jnp.float32
NT = (((1,), (1,)), ((), ()))
LAG = ("z", "y")
PAR = ("x", "core")
VMEM = pl.BlockSpec(memory_space=pltpu.VMEM)


def near(value):
    return pltpu.with_memory_space_constraint(value, pltpu.VMEM)


def call(kernel, out_shape, *args):
    return pl.pallas_call(
        kernel,
        out_shape=out_shape,
        in_specs=[VMEM] * len(args),
        out_specs=jax.tree.map(lambda _: VMEM, out_shape),
        compiler_params=pltpu.CompilerParams(vmem_limit_bytes=6 * 2**20),
    )(*[near(arg) for arg in args])


def shape(*dims):
    return pltpu.VMEM(dims, F32)


def result(*dims):
    return jax.ShapeDtypeStruct(dims, F32)


def tile_zero_kernel(prior, raw, out):
    tile = lax.dot_general(prior[...], raw[...], NT, preferred_element_type=F32)
    for x in range(4):
        for c in range(2):
            first = x * 128 + c * 64
            out[c, x] = tile[first : first + 64]


def tile_one_kernel(prior, raw_next, prior_last, raw, out):
    def form(left, right):
        tile = lax.dot_general(left[...], right[...], NT, preferred_element_type=F32)
        for x in range(4):
            for c in range(2):
                for y in range(4):
                    first = x * 128 + c * 64 + y * 16
                    out[y, x, c] = tile[first : first + 16]

    core = lax.axis_index("core")
    pl.when(core == 0)(lambda: form(prior, raw_next))
    pl.when(core == 1)(lambda: form(prior_last, raw))


def add_kernel(parts, out):
    total = parts[0]
    for i in range(1, parts.shape[0]):
        total = total + parts[i]
    out[...] = total


def spread(ref, half, value, first):
    for i in range(2):
        for j in range(4):
            tile = value[i * 8 : (i + 1) * 8, j * 128 : (j + 1) * 128]
            ref[first + i * 4 + j, half * 8 : (half + 1) * 8, :] = tile


def gathered(ref, half, first):
    rows = []
    for i in range(2):
        tiles = [ref[first + i * 4 + j, half * 8 : (half + 1) * 8, :] for j in range(4)]
        rows.append(jnp.concatenate(tiles, axis=1))
    return jnp.concatenate(rows, axis=0)


def local_prefix_kernel(zero, one, local, ahead):
    total_zero, total_one, delayed = None, None, []
    for lag in range(4):
        here, late = one[lag, 0, 0], one[lag, 0, 1]
        for x in range(1, 4):
            here, late = here + one[lag, x, 0], late + one[lag, x, 1]
        total_zero = zero[lag] if lag == 0 else total_zero + zero[lag]
        local[lag, 0] = total_zero
        if lag == 0:
            spread(ahead, 1, late, 8)
            total_one = here + late
        else:
            local[lag - 1, 1] = total_one + late
            total_one = total_one + here + late
    local[3, 1] = total_one
    spread(ahead, 0, total_zero, 0)
    spread(ahead, 0, total_one, 8)
    spread(ahead, 1, jnp.zeros_like(total_zero), 0)


def lag_scan_kernel(ahead, back):
    state = jnp.zeros((8, 128), F32)
    for z in range(16):
        back[z, 0:8] = state
        state = state + ahead[z, 0:8]
        back[z, 8:16] = ahead[z + 1, 8:16] if z < 15 else jnp.zeros((8, 128), F32)


def finish_kernel(local, back, out):
    earlier_zero, earlier_one, late = gathered(back, 0, 0), gathered(back, 0, 8), gathered(back, 1, 8)
    for lag in range(4):
        out[lag, 0:16] = local[lag, 0] + earlier_zero
        last = local[lag, 1] + earlier_one
        out[lag, 16:32] = last + late if lag == 3 else last


def split_kernel(rows, zero, one):
    for y in range(4):
        zero[0, y * 16 : (y + 1) * 16] = rows[y, 0:16]
        one[0, y * 16 : (y + 1) * 16] = rows[y, 16:32]


def exchange(value, axes):
    return lax.all_to_all(value, axes, 0, 0, tiled=True)


def body(prior_rows, raw_rows):
    prior, raw = prior_rows[0], raw_rows[0]
    device = np.arange(512).reshape(64, 4, 2)
    down = [(int(device[l + 1, x, 0]), int(device[l, x, 0])) for l in range(63) for x in range(4)]
    up = [(int(device[l, x, 1]), int(device[l + 1, x, 1])) for l in range(63) for x in range(4)]
    everyone = LAG + PAR
    raw_next = lax.ppermute(raw, everyone, down)
    prior_last = lax.ppermute(prior, everyone, up)

    zero = call(tile_zero_kernel, shape(2, 4, 64, 512), prior, raw)
    zero = call(add_kernel, shape(4, 64, 512), exchange(zero, "core"))
    zero = call(add_kernel, shape(64, 512), exchange(zero, "x"))
    zero = exchange(zero.reshape(4, 16, 512), "y")

    raw_next, prior_last, zero = lax.optimization_barrier((raw_next, prior_last, zero))
    one = call(tile_one_kernel, shape(4, 4, 2, 16, 512), prior, raw_next, prior_last, raw)
    one = exchange(one.reshape(32, 16, 512), ("y", "x", "core")).reshape(4, 4, 2, 16, 512)

    local, ahead = call(local_prefix_kernel, (shape(4, 2, 16, 512), shape(16, 16, 128)), zero, one)
    back = call(lag_scan_kernel, shape(16, 16, 128), exchange(ahead, "z"))
    rows = call(finish_kernel, shape(4, 32, 512), local, exchange(back, "z"))
    return tuple(call(split_kernel, (result(1, 64, 512), result(1, 64, 512)), exchange(rows, "y")))


def solution(mesh):
    chips = Mesh(mesh.devices.reshape(16, 4, 4, 2), LAG + PAR)
    in_specs = (P(LAG, None, PAR), P(LAG, None, PAR))
    out_specs = (P(LAG, PAR, None), P(LAG, PAR, None))
    return jax.shard_map(body, mesh=chips, in_specs=in_specs, out_specs=out_specs, check_vma=False)
```

```python
import jax
import jax.numpy as jnp
import numpy as np
from jax import lax
from jax.experimental import pallas as pl
from jax.experimental.pallas import tpu as pltpu
from jax.sharding import Mesh, PartitionSpec as P

F32 = jnp.float32
F16 = jnp.float16
NT = (((1,), (1,)), ((), ()))
LAG = ("z", "y")
PAR = ("x", "core")
VMEM = pl.BlockSpec(memory_space=pltpu.VMEM)


def near(value):
    return pltpu.with_memory_space_constraint(value, pltpu.VMEM)


def call(kernel, out_shape, *args):
    return pl.pallas_call(
        kernel,
        out_shape=out_shape,
        in_specs=[VMEM] * len(args),
        out_specs=jax.tree.map(lambda _: VMEM, out_shape),
        compiler_params=pltpu.CompilerParams(vmem_limit_bytes=6 * 2**20),
    )(*[near(arg) for arg in args])


def shape(*dims):
    return pltpu.VMEM(dims, F32)


def result(*dims):
    return jax.ShapeDtypeStruct(dims, F32)


def exponent_of(value):
    top = jnp.max(jnp.max(jnp.abs(value), axis=0, keepdims=True), axis=1, keepdims=True)
    return jnp.floor(jnp.log2(jnp.maximum(top, 1e-30)))


def pack(value, scale, exponent):
    half = value.shape[0] // 2
    sent = value * scale
    tail = jnp.broadcast_to(exponent, (half, 128))
    return jnp.concatenate([sent[:half], sent[half:], tail], axis=1)


def unpack(sent):
    scale = jnp.exp2(sent[:, 1024:] - 14.0)
    scale = jnp.concatenate([scale] * 4, axis=1)
    return sent[:, :512] * scale, sent[:, 512:1024] * scale


def tile_zero_kernel(prior, raw, out):
    tile = lax.dot_general(prior[...], raw[...], NT, preferred_element_type=F32)
    for x in range(4):
        for c in range(2):
            first = x * 128 + c * 64
            out[c, x] = tile[first : first + 64]


def tile_one_kernel(prior, raw_next, prior_last, raw, out):
    def form(left, right):
        tile = lax.dot_general(left[...], right[...], NT, preferred_element_type=F32)
        exponent = exponent_of(tile)
        scale = jnp.exp2(14.0 - exponent)
        for x in range(4):
            for c in range(2):
                for y in range(4):
                    first = x * 128 + c * 64 + y * 16
                    out[y, x, c] = pack(tile[first : first + 16], scale, exponent)

    core = lax.axis_index("core")
    pl.when(core == 0)(lambda: form(prior, raw_next))
    pl.when(core == 1)(lambda: form(prior_last, raw))


def add_cores_kernel(parts, out):
    for x in range(4):
        total = parts[0, x] + parts[1, x]
        exponent = exponent_of(total)
        out[x] = pack(total, jnp.exp2(14.0 - exponent), exponent)


def add_chips_kernel(parts, out):
    out[...] = summed([parts[x] for x in range(4)])


def spread(ref, half, value, first):
    for i in range(2):
        for j in range(4):
            tile = value[i * 8 : (i + 1) * 8, j * 128 : (j + 1) * 128]
            ref[first + i * 4 + j, half * 8 : (half + 1) * 8, :] = tile


def gathered(ref, half, first):
    rows = []
    for i in range(2):
        tiles = [ref[first + i * 4 + j, half * 8 : (half + 1) * 8, :] for j in range(4)]
        rows.append(jnp.concatenate(tiles, axis=1))
    return jnp.concatenate(rows, axis=0)


def summed(parts):
    top, bottom = unpack(parts[0])
    for part in parts[1:]:
        more_top, more_bottom = unpack(part)
        top, bottom = top + more_top, bottom + more_bottom
    return jnp.concatenate([top, bottom], axis=0)


def local_prefix_kernel(zero, one, local, ahead):
    total_zero, total_one, delayed = None, None, []
    for lag in range(4):
        here, late = (summed([one[lag, x, c] for x in range(4)]) for c in range(2))
        total_zero = zero[lag] if lag == 0 else total_zero + zero[lag]
        local[lag, 0] = total_zero
        if lag == 0:
            spread(ahead, 1, late, 8)
            total_one = here + late
        else:
            local[lag - 1, 1] = total_one + late
            total_one = total_one + here + late
    local[3, 1] = total_one
    spread(ahead, 0, total_zero, 0)
    spread(ahead, 0, total_one, 8)
    spread(ahead, 1, jnp.zeros_like(total_zero), 0)


def lag_scan_kernel(ahead, back):
    state = jnp.zeros((8, 128), F32)
    for z in range(16):
        back[z, 0:8] = state
        state = state + ahead[z, 0:8]
        back[z, 8:16] = ahead[z + 1, 8:16] if z < 15 else jnp.zeros((8, 128), F32)


def finish_kernel(local, back, out):
    earlier_zero, earlier_one, late = gathered(back, 0, 0), gathered(back, 0, 8), gathered(back, 1, 8)
    for lag in range(4):
        out[lag, 0:16] = local[lag, 0] + earlier_zero
        last = local[lag, 1] + earlier_one
        out[lag, 16:32] = last + late if lag == 3 else last


def split_kernel(rows, zero, one):
    for y in range(4):
        zero[0, y * 16 : (y + 1) * 16] = rows[y, 0:16]
        one[0, y * 16 : (y + 1) * 16] = rows[y, 16:32]


def exchange(value, axes):
    return lax.all_to_all(value, axes, 0, 0, tiled=True)


def exchange_short(value, axes):
    return exchange(value.astype(F16), axes).astype(F32)


def body(prior_rows, raw_rows):
    prior, raw = prior_rows[0], raw_rows[0]
    device = np.arange(512).reshape(64, 4, 2)
    down = [(int(device[l + 1, x, 0]), int(device[l, x, 0])) for l in range(63) for x in range(4)]
    up = [(int(device[l, x, 1]), int(device[l + 1, x, 1])) for l in range(63) for x in range(4)]
    everyone = LAG + PAR
    raw_next = lax.ppermute(raw, everyone, down)
    prior_last = lax.ppermute(prior, everyone, up)

    zero = call(tile_zero_kernel, shape(2, 4, 64, 512), prior, raw)
    zero = call(add_cores_kernel, shape(4, 32, 1152), exchange(zero, "core"))
    zero = call(add_chips_kernel, shape(64, 512), exchange_short(zero, "x"))
    zero = exchange(zero.reshape(4, 16, 512), "y")

    raw_next, prior_last, zero = lax.optimization_barrier((raw_next, prior_last, zero))
    one = call(tile_one_kernel, shape(4, 4, 2, 8, 1152), prior, raw_next, prior_last, raw)
    one = exchange_short(one.reshape(32, 8, 1152), ("y", "x", "core")).reshape(4, 4, 2, 8, 1152)

    local, ahead = call(local_prefix_kernel, (shape(4, 2, 16, 512), shape(16, 16, 128)), zero, one)
    back = call(lag_scan_kernel, shape(16, 16, 128), exchange(ahead, "z"))
    rows = call(finish_kernel, shape(4, 32, 512), local, exchange(back, "z"))
    return tuple(call(split_kernel, (result(1, 64, 512), result(1, 64, 512)), exchange(rows, "y")))


def solution(mesh):
    chips = Mesh(mesh.devices.reshape(16, 4, 4, 2), LAG + PAR)
    in_specs = (P(LAG, None, PAR), P(LAG, None, PAR))
    out_specs = (P(LAG, PAR, None), P(LAG, PAR, None))
    return jax.shard_map(body, mesh=chips, in_specs=in_specs, out_specs=out_specs, check_vma=False)
```

```python
import jax
import jax.numpy as jnp
import numpy as np
from jax import lax
from jax.experimental import pallas as pl
from jax.experimental.pallas import tpu as pltpu
from jax.sharding import Mesh, PartitionSpec as P

F32 = jnp.float32
F16 = jnp.float16
NT = (((1,), (1,)), ((), ()))
LAG = ("zh", "zl", "y")
PAR = ("x", "core")
VMEM = pl.BlockSpec(memory_space=pltpu.VMEM)
STEPS = 4


def near(value):
    return pltpu.with_memory_space_constraint(value, pltpu.VMEM)


def far(value):
    return pltpu.with_memory_space_constraint(value, pltpu.HBM)


def call(kernel, out_shape, *args):
    return pl.pallas_call(
        kernel,
        out_shape=out_shape,
        in_specs=[VMEM] * len(args),
        out_specs=jax.tree.map(lambda _: VMEM, out_shape),
        compiler_params=pltpu.CompilerParams(vmem_limit_bytes=6 * 2**20),
    )(*[near(arg) for arg in args])


def shape(*dims):
    return pltpu.VMEM(dims, F32)


def result(*dims):
    return jax.ShapeDtypeStruct(dims, F32)


def exponent_of(value):
    top = jnp.max(jnp.max(jnp.abs(value), axis=0, keepdims=True), axis=1, keepdims=True)
    return jnp.floor(jnp.log2(jnp.maximum(top, 1e-30)))


def pack(tile, out):
    exponent = exponent_of(tile)
    tail = jnp.broadcast_to(exponent, (8, 128))
    sent = tile * jnp.exp2(14.0 - exponent)
    for x in range(4):
        for c in range(2):
            for y in range(4):
                first = x * 128 + c * 64 + y * 16
                top, bottom = sent[first : first + 8], sent[first + 8 : first + 16]
                out[y, x, c] = jnp.concatenate([top, bottom, tail], axis=1)


def unpack(sent):
    scale = jnp.exp2(sent[:, 1024:] - 14.0)
    scale = jnp.concatenate([scale] * 4, axis=1)
    return sent[:, :512] * scale, sent[:, 512:1024] * scale


def summed(parts):
    top, bottom = unpack(parts[0])
    for part in parts[1:]:
        more_top, more_bottom = unpack(part)
        top, bottom = top + more_top, bottom + more_bottom
    return jnp.concatenate([top, bottom], axis=0)


def tile_zero_kernel(prior, raw, out, total):
    step = pl.program_id(0)
    part = lax.dot_general(prior[...], raw[...], NT, preferred_element_type=F32)

    @pl.when(step == 0)
    def _():
        total[...] = part

    @pl.when(step > 0)
    def _():
        total[...] += part

    @pl.when(step == STEPS - 1)
    def _():
        pack(total[...], out)


def tile_one_kernel(prior, raw_next, prior_last, raw, out):
    def form(left, right):
        pack(lax.dot_general(left[...], right[...], NT, preferred_element_type=F32), out)

    core = lax.axis_index("core")
    pl.when(core == 0)(lambda: form(prior, raw_next))
    pl.when(core == 1)(lambda: form(prior_last, raw))


def plane_prefix_kernel(zero, one, out):
    def put(first, value):
        for i in range(4):
            out[i, first : first + 16] = value[:, i * 128 : (i + 1) * 128]

    total_zero, total_one = None, None
    for lag in range(4):
        here = summed([zero[lag, x, c] for x in range(4) for c in range(2)])
        total_zero = here if lag == 0 else total_zero + here
        put(lag * 32, total_zero)
        here, late = (summed([one[lag, x, c] for x in range(4)]) for c in range(2))
        if lag == 0:
            put(128, late)
            total_one = here + late
        else:
            put((lag - 1) * 32 + 16, total_one + late)
            total_one = total_one + here + late
    put(3 * 32 + 16, total_one)


def block_prefix_kernel(planes, local, total):
    state = jnp.zeros((32, 128), F32)
    for zl in range(4):
        for lag in range(4):
            here = planes[zl, lag * 32 : (lag + 1) * 32] + state
            local[zl * 4 + lag, 0:16] = here[0:16]
            if lag == 3 and zl < 3:
                local[zl * 4 + lag, 16:32] = here[16:32] + planes[zl + 1, 128:144]
            else:
                local[zl * 4 + lag, 16:32] = here[16:32]
        state = here
    for i in range(4):
        total[i, 0:32] = state
        total[i, 32:48] = planes[0, 128:144]


def finish_kernel(local, total, out):
    place = lax.axis_index("zh")
    earlier, late = jnp.zeros((32, 128), F32), jnp.zeros((16, 128), F32)
    for z in range(4):
        earlier = earlier + jnp.where(z < place, total[z, 0:32], 0.0)
        late = late + jnp.where(z == place + 1, total[z, 32:48], 0.0)
    for i in range(16):
        out[i] = local[i] + earlier
    out[15, 16:32] = local[15, 16:32] + earlier[16:32] + late


def split_kernel(rows, zero, one):
    for zl in range(4):
        for y in range(4):
            here, there = slice(y * 16, (y + 1) * 16), slice(zl * 128, (zl + 1) * 128)
            zero[0, here, there] = rows[zl * 4 + y, 0:16]
            one[0, here, there] = rows[zl * 4 + y, 16:32]


def exchange(value, axes):
    return lax.all_to_all(value, axes, 0, 0, tiled=True)


def reduce_rows(tile):
    tile = exchange(tile.reshape(32, 8, 1152).astype(F16), ("y", "x", "core"))
    return tile.astype(F32).reshape(4, 4, 2, 8, 1152)


def body(prior_rows, raw_rows):
    prior, raw = prior_rows[0], raw_rows[0]
    device = np.arange(512).reshape(64, 4, 2)
    down = [(int(device[l + 1, x, 0]), int(device[l, x, 0])) for l in range(63) for x in range(4)]
    up = [(int(device[l, x, 1]), int(device[l + 1, x, 1])) for l in range(63) for x in range(4)]
    raw_next = lax.ppermute(raw, LAG + PAR, down)
    prior_last = lax.ppermute(prior, LAG + PAR, up)

    sent = shape(4, 4, 2, 8, 1152)
    piece = pl.BlockSpec((512, 2048 // STEPS), lambda step: (0, step))
    zero = pl.pallas_call(
        tile_zero_kernel,
        out_shape=sent,
        grid=(STEPS,),
        in_specs=[piece, piece],
        out_specs=VMEM,
        scratch_shapes=[pltpu.VMEM((512, 512), F32)],
        compiler_params=pltpu.CompilerParams(vmem_limit_bytes=8 * 2**20),
    )(far(prior), far(raw))
    zero = reduce_rows(zero)

    raw_next, prior_last, zero = lax.optimization_barrier((raw_next, prior_last, zero))
    one = reduce_rows(call(tile_one_kernel, sent, prior, raw_next, prior_last, raw))

    planes = exchange(call(plane_prefix_kernel, shape(4, 144, 128), zero, one), "zl")
    local, total = call(block_prefix_kernel, (shape(16, 32, 128), shape(4, 48, 128)), planes)
    rows = call(finish_kernel, shape(16, 32, 128), local, exchange(total, "zh"))
    return tuple(call(split_kernel, (result(1, 64, 512), result(1, 64, 512)), exchange(rows, ("zl", "y"))))


def solution(mesh):
    chips = Mesh(mesh.devices.reshape(4, 4, 4, 4, 2), LAG + PAR)
    in_specs = (P(LAG, None, PAR), P(LAG, None, PAR))
    out_specs = (P(LAG, PAR, None), P(LAG, PAR, None))
    return jax.shard_map(body, mesh=chips, in_specs=in_specs, out_specs=out_specs, check_vma=False)
```

```python
import jax
import jax.numpy as jnp
import numpy as np
from jax import lax
from jax.experimental import pallas as pl
from jax.experimental.pallas import tpu as pltpu
from jax.sharding import Mesh, PartitionSpec as P

F32 = jnp.float32
F16 = jnp.float16
NT = (((1,), (1,)), ((), ()))
LAG = ("zh", "zl", "y")
PAR = ("x", "core")
VMEM = pl.BlockSpec(memory_space=pltpu.VMEM)
STEPS = 4


def near(value):
    return pltpu.with_memory_space_constraint(value, pltpu.VMEM)


def far(value):
    return pltpu.with_memory_space_constraint(value, pltpu.HBM)


def call(kernel, out_shape, *args):
    return pl.pallas_call(
        kernel,
        out_shape=out_shape,
        in_specs=[VMEM] * len(args),
        out_specs=jax.tree.map(lambda _: VMEM, out_shape),
        compiler_params=pltpu.CompilerParams(vmem_limit_bytes=6 * 2**20),
    )(*[near(arg) for arg in args])


def shape(*dims):
    return pltpu.VMEM(dims, F32)


def result(*dims):
    return jax.ShapeDtypeStruct(dims, F32)


def exponent_of(value):
    top = jnp.max(jnp.max(jnp.abs(value), axis=0, keepdims=True), axis=1, keepdims=True)
    return jnp.floor(jnp.log2(jnp.maximum(top, 1e-30)))


def pack(tile, out):
    exponent = exponent_of(tile)
    tail = jnp.broadcast_to(exponent, (8, 128))
    sent = tile * jnp.exp2(14.0 - exponent)
    for x in range(4):
        for c in range(2):
            first = x * 128 + c * 64
            groups = [sent[first + i * 8 : first + (i + 1) * 8] for i in range(8)]
            out[x, c] = jnp.concatenate(groups + [tail], axis=1)


def summed(parts):
    groups = [None] * 8
    for part in parts:
        scale = jnp.exp2(part[:, 4096:] - 14.0)
        scale = jnp.concatenate([scale] * 4, axis=1)
        for i in range(8):
            group = part[:, i * 512 : (i + 1) * 512] * scale
            groups[i] = group if groups[i] is None else groups[i] + group
    return jnp.concatenate(groups, axis=0)


def tile_zero_kernel(prior, raw, out, total):
    step = pl.program_id(0)
    part = lax.dot_general(prior[...], raw[...], NT, preferred_element_type=F32)

    @pl.when(step == 0)
    def _():
        total[...] = part

    @pl.when(step > 0)
    def _():
        total[...] += part

    @pl.when(step == STEPS - 1)
    def _():
        pack(total[...], out)


def tile_one_kernel(prior, raw_next, prior_last, raw, out):
    def form(left, right):
        pack(lax.dot_general(left[...], right[...], NT, preferred_element_type=F32), out)

    core = lax.axis_index("core")
    pl.when(core == 0)(lambda: form(prior, raw_next))
    pl.when(core == 1)(lambda: form(prior_last, raw))


def spread_kernel(zero, one, out):
    whole = summed([zero[x, c] for x in range(4) for c in range(2)])
    here, late = (summed([one[x, c] for x in range(4)]) for c in range(2))
    for i, value in enumerate((whole, here, late)):
        for zl in range(4):
            for y in range(4):
                out[zl * 4 + y, i * 16 : (i + 1) * 16] = value[y * 16 : (y + 1) * 16, zl * 128 : (zl + 1) * 128]


def block_prefix_kernel(lags, local, total):
    zero, one = jnp.zeros((16, 128), F32), jnp.zeros((16, 128), F32)
    for lag in range(16):
        zero = zero + lags[lag, 0:16]
        one = one + lags[lag, 16:32] + lags[lag, 32:48]
        local[lag, 0:16] = zero
        local[lag, 16:32] = one + lags[lag + 1, 32:48] if lag < 15 else one
    for i in range(4):
        total[i, 0:16] = zero
        total[i, 16:32] = one
        total[i, 32:48] = lags[0, 32:48]


def finish_kernel(local, total, out):
    place = lax.axis_index("zh")
    earlier, late = jnp.zeros((32, 128), F32), jnp.zeros((16, 128), F32)
    for z in range(4):
        earlier = earlier + jnp.where(z < place, total[z, 0:32], 0.0)
        late = late + jnp.where(z == place + 1, total[z, 32:48], 0.0)
    for i in range(16):
        out[i] = local[i] + earlier
    out[15, 16:32] = local[15, 16:32] + earlier[16:32] + late


def split_kernel(rows, zero, one):
    for zl in range(4):
        for y in range(4):
            here, there = slice(y * 16, (y + 1) * 16), slice(zl * 128, (zl + 1) * 128)
            zero[0, here, there] = rows[zl * 4 + y, 0:16]
            one[0, here, there] = rows[zl * 4 + y, 16:32]


def exchange(value, axes):
    return lax.all_to_all(value, axes, 0, 0, tiled=True)


def reduce_rows(tile):
    tile = exchange(tile.reshape(8, 8, 4224).astype(F16), PAR)
    return tile.astype(F32).reshape(4, 2, 8, 4224)


def body(prior_rows, raw_rows):
    prior, raw = prior_rows[0], raw_rows[0]
    device = np.arange(512).reshape(64, 4, 2)
    down = [(int(device[l + 1, x, 0]), int(device[l, x, 0])) for l in range(63) for x in range(4)]
    up = [(int(device[l, x, 1]), int(device[l + 1, x, 1])) for l in range(63) for x in range(4)]
    raw_next = lax.ppermute(raw, LAG + PAR, down)
    prior_last = lax.ppermute(prior, LAG + PAR, up)

    sent = shape(4, 2, 8, 4224)
    piece = pl.BlockSpec((512, 2048 // STEPS), lambda step: (0, step))
    zero = pl.pallas_call(
        tile_zero_kernel,
        out_shape=sent,
        grid=(STEPS,),
        in_specs=[piece, piece],
        out_specs=VMEM,
        scratch_shapes=[pltpu.VMEM((512, 512), F32)],
        compiler_params=pltpu.CompilerParams(vmem_limit_bytes=8 * 2**20),
    )(far(prior), far(raw))
    zero = reduce_rows(zero)

    raw_next, prior_last, zero = lax.optimization_barrier((raw_next, prior_last, zero))
    one = reduce_rows(call(tile_one_kernel, sent, prior, raw_next, prior_last, raw))

    lags = exchange(call(spread_kernel, shape(16, 48, 128), zero, one), ("zl", "y"))
    local, total = call(block_prefix_kernel, (shape(16, 32, 128), shape(4, 48, 128)), lags)
    rows = call(finish_kernel, shape(16, 32, 128), local, exchange(total, "zh"))
    return tuple(call(split_kernel, (result(1, 64, 512), result(1, 64, 512)), exchange(rows, ("zl", "y"))))


def solution(mesh):
    chips = Mesh(mesh.devices.reshape(4, 4, 4, 4, 2), LAG + PAR)
    in_specs = (P(LAG, None, PAR), P(LAG, None, PAR))
    out_specs = (P(LAG, PAR, None), P(LAG, PAR, None))
    return jax.shard_map(body, mesh=chips, in_specs=in_specs, out_specs=out_specs, check_vma=False)
```

```python
import jax
import jax.numpy as jnp
import numpy as np
from jax import lax
from jax.experimental import pallas as pl
from jax.experimental.pallas import tpu as pltpu
from jax.sharding import Mesh, PartitionSpec as P

F32 = jnp.float32
F16 = jnp.float16
NT = (((1,), (1,)), ((), ()))
LAG = ("zh", "zl", "y")
PAR = ("x", "core")
VMEM = pl.BlockSpec(memory_space=pltpu.VMEM)
STEPS = 4


def near(value):
    return pltpu.with_memory_space_constraint(value, pltpu.VMEM)


def far(value):
    return pltpu.with_memory_space_constraint(value, pltpu.HBM)


def call(kernel, out_shape, *args):
    return pl.pallas_call(
        kernel,
        out_shape=out_shape,
        in_specs=[VMEM] * len(args),
        out_specs=jax.tree.map(lambda _: VMEM, out_shape),
        compiler_params=pltpu.CompilerParams(vmem_limit_bytes=6 * 2**20),
    )(*[near(arg) for arg in args])


def shape(*dims):
    return pltpu.VMEM(dims, F32)


def result(*dims):
    return jax.ShapeDtypeStruct(dims, F32)


def exponent_of(value):
    top = jnp.max(jnp.max(jnp.abs(value), axis=0, keepdims=True), axis=1, keepdims=True)
    return jnp.floor(jnp.log2(jnp.maximum(top, 1e-30)))


LEVEL = 3.3


def encode(value, exponent):
    size = jnp.abs(value) * jnp.exp2(7.0 - exponent)
    binade = jnp.floor(jnp.log2(jnp.maximum(size, 1.0)))
    place = LEVEL * (binade + size * jnp.exp2(-binade))
    whole = jnp.floor(place)
    code = jnp.exp2(whole - 14.0) * (1.0 + (place - whole))
    return jnp.where(value < 0, -code, code)


def decode(code, exponent):
    size = jnp.abs(code)
    whole = jnp.floor(jnp.log2(jnp.maximum(size, 2.0**-14)))
    place = (whole + 13.0 + size * jnp.exp2(-whole)) * (1.0 / LEVEL)
    binade = jnp.maximum(jnp.floor(place) - 1.0, 0.0)
    value = (place - binade) * jnp.exp2(binade + exponent - 7.0)
    return jnp.where(code < 0, -value, value)


def pack(tile, out):
    exponent = exponent_of(tile)
    tail = jnp.broadcast_to(exponent, (8, 128))
    sent = tile * jnp.exp2(14.0 - exponent)
    for x in range(4):
        for c in range(2):
            first = x * 128 + c * 64
            groups = [sent[first + i * 8 : first + (i + 1) * 8] for i in range(8)]
            out[x, c] = jnp.concatenate(groups + [tail], axis=1)


def summed(parts):
    groups = [None] * 8
    for part in parts:
        scale = jnp.exp2(part[:, 4096:] - 14.0)
        scale = jnp.concatenate([scale] * 4, axis=1)
        for i in range(8):
            group = part[:, i * 512 : (i + 1) * 512] * scale
            groups[i] = group if groups[i] is None else groups[i] + group
    return jnp.concatenate(groups, axis=0)


def tile_zero_kernel(prior, raw, out, total):
    step = pl.program_id(0)
    part = lax.dot_general(prior[...], raw[...], NT, preferred_element_type=F32)

    @pl.when(step == 0)
    def _():
        total[...] = part

    @pl.when(step > 0)
    def _():
        total[...] += part

    @pl.when(step == STEPS - 1)
    def _():
        pack(total[...], out)


def tile_one_kernel(prior, raw_next, prior_last, raw, out):
    def form(left, right):
        pack(lax.dot_general(left[...], right[...], NT, preferred_element_type=F32), out)

    core = lax.axis_index("core")
    pl.when(core == 0)(lambda: form(prior, raw_next))
    pl.when(core == 1)(lambda: form(prior_last, raw))


def spread_kernel(zero, one, out):
    whole = summed([zero[x, c] for x in range(4) for c in range(2)])
    here, late = (summed([one[x, c] for x in range(4)]) for c in range(2))
    for i, value in enumerate((whole, here, late)):
        exponent = exponent_of(value)
        value = encode(value, exponent)
        for zl in range(4):
            for y in range(4):
                out[zl * 4 + y, i * 16 : (i + 1) * 16] = value[y * 16 : (y + 1) * 16, zl * 128 : (zl + 1) * 128]
                out[zl * 4 + y, 48 + i * 8 : 56 + i * 8] = jnp.broadcast_to(exponent, (8, 128))


def block_prefix_kernel(lags, local, total):
    def read(lag, i):
        exponent = lags[lag, 48 + i * 8 : 56 + i * 8]
        exponent = jnp.concatenate([exponent, exponent], axis=0)
        return decode(lags[lag, i * 16 : (i + 1) * 16], exponent)

    zero, one = jnp.zeros((16, 128), F32), jnp.zeros((16, 128), F32)
    lates = [read(lag, 2) for lag in range(16)]
    for lag in range(16):
        zero = zero + read(lag, 0)
        one = one + read(lag, 1) + lates[lag]
        local[lag, 0:16] = zero
        local[lag, 16:32] = one + lates[lag + 1] if lag < 15 else one
    for i in range(4):
        total[i, 0:16] = zero
        total[i, 16:32] = one
        total[i, 32:48] = lates[0]


def finish_kernel(local, total, out):
    place = lax.axis_index("zh")
    earlier, late = jnp.zeros((32, 128), F32), jnp.zeros((16, 128), F32)
    for z in range(4):
        earlier = earlier + jnp.where(z < place, total[z, 0:32], 0.0)
        late = late + jnp.where(z == place + 1, total[z, 32:48], 0.0)
    rows = [local[i] + earlier for i in range(16)]
    rows[15] = jnp.concatenate([rows[15][0:16], rows[15][16:32] + late], axis=0)
    for i in range(2):
        part = jnp.concatenate([row[i * 16 : (i + 1) * 16] for row in rows], axis=0)
        exponent = exponent_of(part)
        part = encode(part, exponent)
        for lag in range(16):
            out[lag, i * 16 : (i + 1) * 16] = part[lag * 16 : (lag + 1) * 16]
            out[lag, 32 + i * 8 : 40 + i * 8] = jnp.broadcast_to(exponent, (8, 128))


def split_kernel(rows, zero, one):
    for zl in range(4):
        for y in range(4):
            here, there = slice(y * 16, (y + 1) * 16), slice(zl * 128, (zl + 1) * 128)
            for i, out in enumerate((zero, one)):
                exponent = rows[zl * 4 + y, 32 + i * 8 : 40 + i * 8]
                exponent = jnp.concatenate([exponent, exponent], axis=0)
                out[0, here, there] = decode(rows[zl * 4 + y, i * 16 : (i + 1) * 16], exponent)


def exchange(value, axes):
    return lax.all_to_all(value, axes, 0, 0, tiled=True)


def exchange_short(value, axes):
    return exchange(value.astype(F16), axes).astype(F32)


def reduce_rows(tile):
    return exchange_short(tile.reshape(8, 8, 4224), PAR).reshape(4, 2, 8, 4224)


def body(prior_rows, raw_rows):
    prior, raw = prior_rows[0], raw_rows[0]
    device = np.arange(512).reshape(64, 4, 2)
    down = [(int(device[l + 1, x, 0]), int(device[l, x, 0])) for l in range(63) for x in range(4)]
    up = [(int(device[l, x, 1]), int(device[l + 1, x, 1])) for l in range(63) for x in range(4)]
    raw_next = lax.ppermute(raw, LAG + PAR, down)
    prior_last = lax.ppermute(prior, LAG + PAR, up)

    sent = shape(4, 2, 8, 4224)
    piece = pl.BlockSpec((512, 2048 // STEPS), lambda step: (0, step))
    zero = pl.pallas_call(
        tile_zero_kernel,
        out_shape=sent,
        grid=(STEPS,),
        in_specs=[piece, piece],
        out_specs=VMEM,
        scratch_shapes=[pltpu.VMEM((512, 512), F32)],
        compiler_params=pltpu.CompilerParams(vmem_limit_bytes=8 * 2**20),
    )(far(prior), far(raw))
    zero = reduce_rows(zero)

    raw_next, prior_last, zero = lax.optimization_barrier((raw_next, prior_last, zero))
    one = reduce_rows(call(tile_one_kernel, sent, prior, raw_next, prior_last, raw))

    lags = exchange_short(call(spread_kernel, shape(16, 72, 128), zero, one), ("zl", "y"))
    local, total = call(block_prefix_kernel, (shape(16, 32, 128), shape(4, 48, 128)), lags)
    rows = call(finish_kernel, shape(16, 48, 128), local, exchange(total, "zh"))
    rows = exchange_short(rows, ("zl", "y"))
    return tuple(call(split_kernel, (result(1, 64, 512), result(1, 64, 512)), rows))


def solution(mesh):
    chips = Mesh(mesh.devices.reshape(4, 4, 4, 4, 2), LAG + PAR)
    in_specs = (P(LAG, None, PAR), P(LAG, None, PAR))
    out_specs = (P(LAG, PAR, None), P(LAG, PAR, None))
    return jax.shard_map(body, mesh=chips, in_specs=in_specs, out_specs=out_specs, check_vma=False)
```

```python
import jax
import jax.numpy as jnp
import numpy as np
from jax import lax
from jax.experimental import pallas as pl
from jax.experimental.pallas import tpu as pltpu
from jax.sharding import Mesh, PartitionSpec as P

F32 = jnp.float32
F16 = jnp.float16
NT = (((1,), (1,)), ((), ()))
LAG = ("zh", "zl", "y")
PAR = ("x", "core")
VMEM = pl.BlockSpec(memory_space=pltpu.VMEM)


def near(value):
    return pltpu.with_memory_space_constraint(value, pltpu.VMEM)


def call(kernel, out_shape, *args):
    return pl.pallas_call(
        kernel,
        out_shape=out_shape,
        in_specs=[VMEM] * len(args),
        out_specs=jax.tree.map(lambda _: VMEM, out_shape),
        compiler_params=pltpu.CompilerParams(vmem_limit_bytes=6 * 2**20),
    )(*[near(arg) for arg in args])


def shape(*dims):
    return pltpu.VMEM(dims, F32)


def result(*dims):
    return jax.ShapeDtypeStruct(dims, F32)


def exponent_of(value):
    top = jnp.max(jnp.max(jnp.abs(value), axis=0, keepdims=True), axis=1, keepdims=True)
    return jnp.floor(jnp.log2(jnp.maximum(top, 1e-30)))


LEVEL = 3.3


def encode(value, exponent):
    size = jnp.abs(value) * jnp.exp2(7.0 - exponent)
    binade = jnp.floor(jnp.log2(jnp.maximum(size, 1.0)))
    place = LEVEL * (binade + size * jnp.exp2(-binade))
    whole = jnp.floor(place)
    code = jnp.exp2(whole - 14.0) * (1.0 + (place - whole))
    return jnp.where(value < 0, -code, code)


def decode(code, exponent):
    size = jnp.abs(code)
    whole = jnp.floor(jnp.log2(jnp.maximum(size, 2.0**-14)))
    place = (whole + 13.0 + size * jnp.exp2(-whole)) * (1.0 / LEVEL)
    binade = jnp.maximum(jnp.floor(place) - 1.0, 0.0)
    value = (place - binade) * jnp.exp2(binade + exponent - 7.0)
    return jnp.where(code < 0, -value, value)


def pack(tile, height, out):
    exponent = exponent_of(tile)
    tail = jnp.broadcast_to(exponent, (8, 128))
    sent = tile * jnp.exp2(14.0 - exponent)
    for owner in range(8):
        groups = [sent[first : first + 8] for first in range(owner * height, (owner + 1) * height, 8)]
        out[owner] = jnp.concatenate(groups + [tail], axis=1)


def summed(parts, width):
    lanes = parts[0].shape[1] - 128
    groups = [None] * (lanes // width)
    for part in parts:
        scale = jnp.exp2(part[:, lanes:] - 14.0)
        scale = jnp.concatenate([scale] * (width // 128), axis=1)
        for i in range(len(groups)):
            group = part[:, i * width : (i + 1) * width] * scale
            groups[i] = group if groups[i] is None else groups[i] + group
    return jnp.concatenate(groups, axis=0)


def picked(prior, raw, half, out, sems):
    def copies(source, first, step):
        rows = [(source.at[pl.ds(first + i * step, 32)], out.at[pl.ds(i * 32, 32)]) for i in range(8)]
        return [pltpu.make_async_copy(here, there, sems.at[i]) for i, (here, there) in enumerate(rows)]

    return copies(raw, half * 256, 32), copies(prior, half * 32, 64)


def run(copies):
    for copy in copies:
        copy.start()
    for copy in copies:
        copy.wait()


def first_half_kernel(prior, raw, out, sems):
    from_raw, from_prior = picked(prior, raw, 0, out, sems)
    core = lax.axis_index("core")
    pl.when(core == 0)(lambda: run(from_raw))
    pl.when(core == 1)(lambda: run(from_prior))


def second_half_kernel(prior, raw, out, prior_near, raw_near, sems):
    from_raw, from_prior = picked(prior, raw, 1, out, sems)
    whole = []
    for i in range(4):
        rows = pl.ds(i * 128, 128)
        whole.append(pltpu.make_async_copy(prior.at[rows], prior_near.at[rows], sems.at[8 + i]))
        whole.append(pltpu.make_async_copy(raw.at[rows], raw_near.at[rows], sems.at[12 + i]))
    core = lax.axis_index("core")
    pl.when(core == 0)(lambda: run(from_raw + whole))
    pl.when(core == 1)(lambda: run(from_prior + whole))


def fetch(kernel, out_shape, copies, prior, raw):
    far = [pltpu.with_memory_space_constraint(value, pltpu.HBM) for value in (prior, raw)]
    return pl.pallas_call(
        kernel,
        out_shape=out_shape,
        in_specs=[pl.BlockSpec(memory_space=pltpu.HBM)] * 2,
        out_specs=jax.tree.map(lambda _: VMEM, out_shape),
        scratch_shapes=[pltpu.SemaphoreType.DMA((copies,))],
        compiler_params=pltpu.CompilerParams(vmem_limit_bytes=2 * 2**20),
    )(*far)


def tile_zero_kernel(prior, raw, out):
    pack(lax.dot_general(prior[...], raw[...], NT, preferred_element_type=F32), 64, out)


def tile_one_kernel(prior, raw, moved, out):
    def form(left, right, height):
        pack(lax.dot_general(left[...], right[...], NT, preferred_element_type=F32), height, out)

    core = lax.axis_index("core")
    pl.when(core == 0)(lambda: form(prior, moved, 64))
    pl.when(core == 1)(lambda: form(moved, raw, 32))


def spread_kernel(zero, one_a, one_b, out):
    whole = summed([zero[i] for i in range(8)], 512)
    here = jnp.concatenate([summed([one[i] for i in range(0, 8, 2)], 256) for one in (one_a, one_b)], axis=1)
    late = jnp.concatenate([summed([one[i] for i in range(1, 8, 2)], 512) for one in (one_a, one_b)], axis=0)
    for i, value in enumerate((whole, here, late)):
        exponent = exponent_of(value)
        value = encode(value, exponent)
        for zl in range(4):
            for y in range(4):
                out[zl * 4 + y, i * 16 : (i + 1) * 16] = value[y * 16 : (y + 1) * 16, zl * 128 : (zl + 1) * 128]
                out[zl * 4 + y, 48 + i * 8 : 56 + i * 8] = jnp.broadcast_to(exponent, (8, 128))


def block_prefix_kernel(lags, local, total):
    def read(lag, i):
        exponent = lags[lag, 48 + i * 8 : 56 + i * 8]
        exponent = jnp.concatenate([exponent, exponent], axis=0)
        return decode(lags[lag, i * 16 : (i + 1) * 16], exponent)

    zero, one = jnp.zeros((16, 128), F32), jnp.zeros((16, 128), F32)
    lates = [read(lag, 2) for lag in range(16)]
    for lag in range(16):
        zero = zero + read(lag, 0)
        one = one + read(lag, 1) + lates[lag]
        local[lag, 0:16] = zero
        local[lag, 16:32] = one + lates[lag + 1] if lag < 15 else one
    for i in range(4):
        total[i, 0:16] = zero
        total[i, 16:32] = one
        total[i, 32:48] = lates[0]


def finish_kernel(local, total, out):
    place = lax.axis_index("zh")
    earlier, late = jnp.zeros((32, 128), F32), jnp.zeros((16, 128), F32)
    for z in range(4):
        earlier = earlier + jnp.where(z < place, total[z, 0:32], 0.0)
        late = late + jnp.where(z == place + 1, total[z, 32:48], 0.0)
    for i in range(16):
        out[i] = local[i] + earlier
    out[15, 16:32] = local[15, 16:32] + earlier[16:32] + late


def split_kernel(rows, zero, one):
    for zl in range(4):
        for y in range(4):
            here, there = slice(y * 16, (y + 1) * 16), slice(zl * 128, (zl + 1) * 128)
            zero[0, here, there] = rows[zl * 4 + y, 0:16]
            one[0, here, there] = rows[zl * 4 + y, 16:32]


def exchange(value, axes):
    return lax.all_to_all(value, axes, 0, 0, tiled=True)


def exchange_short(value, axes):
    return exchange(value.astype(F16), axes).astype(F32)


def body(prior_rows, raw_rows):
    prior, raw = prior_rows[0], raw_rows[0]
    device = np.arange(512).reshape(64, 4, 2)
    down = [(int(device[l + 1, x, 0]), int(device[l, x, 0])) for l in range(63) for x in range(4)]
    up = [(int(device[l, x, 1]), int(device[l + 1, x, 1])) for l in range(63) for x in range(4)]

    half = pltpu.VMEM((256, 2048), jnp.bfloat16)
    full = pltpu.VMEM((512, 2048), jnp.bfloat16)
    sent = fetch(first_half_kernel, half, 8, prior, raw)
    moved_a = lax.ppermute(sent, LAG + PAR, down + up)
    sent, prior, raw = fetch(second_half_kernel, (half, full, full), 16, prior, raw)
    moved_b = lax.ppermute(sent, LAG + PAR, down + up)

    zero = exchange_short(call(tile_zero_kernel, shape(8, 8, 4224), prior, raw), PAR)
    moved_a, zero = lax.optimization_barrier((moved_a, zero))
    one_a = exchange_short(call(tile_one_kernel, shape(8, 8, 2176), prior, raw, moved_a), PAR)
    moved_b, one_a = lax.optimization_barrier((moved_b, one_a))
    one_b = exchange_short(call(tile_one_kernel, shape(8, 8, 2176), prior, raw, moved_b), PAR)

    lags = exchange_short(call(spread_kernel, shape(16, 72, 128), zero, one_a, one_b), ("zl", "y"))
    local, total = call(block_prefix_kernel, (shape(16, 32, 128), shape(4, 48, 128)), lags)
    rows = call(finish_kernel, shape(16, 32, 128), local, exchange(total, "zh"))
    return tuple(call(split_kernel, (result(1, 64, 512), result(1, 64, 512)), exchange(rows, ("zl", "y"))))


def solution(mesh):
    chips = Mesh(mesh.devices.reshape(4, 4, 4, 4, 2), LAG + PAR)
    in_specs = (P(LAG, None, PAR), P(LAG, None, PAR))
    out_specs = (P(LAG, PAR, None), P(LAG, PAR, None))
    return jax.shard_map(body, mesh=chips, in_specs=in_specs, out_specs=out_specs, check_vma=False)
```

```python
import jax
import jax.numpy as jnp
import numpy as np
from jax import lax
from jax.experimental import pallas as pl
from jax.experimental.pallas import tpu as pltpu
from jax.sharding import Mesh, PartitionSpec as P

F32 = jnp.float32
F16 = jnp.float16
NT = (((1,), (1,)), ((), ()))
LAG = ("zh", "zl", "y")
PAR = ("x", "core")
VMEM = pl.BlockSpec(memory_space=pltpu.VMEM)
STEPS = 4


def near(value):
    return pltpu.with_memory_space_constraint(value, pltpu.VMEM)


def far(value):
    return pltpu.with_memory_space_constraint(value, pltpu.HBM)


def call(kernel, out_shape, *args):
    return pl.pallas_call(
        kernel,
        out_shape=out_shape,
        in_specs=[VMEM] * len(args),
        out_specs=jax.tree.map(lambda _: VMEM, out_shape),
        compiler_params=pltpu.CompilerParams(vmem_limit_bytes=6 * 2**20),
    )(*[near(arg) for arg in args])


def shape(*dims):
    return pltpu.VMEM(dims, F32)


def result(*dims):
    return jax.ShapeDtypeStruct(dims, F32)


def exponent_of(value):
    top = jnp.max(jnp.max(jnp.abs(value), axis=0, keepdims=True), axis=1, keepdims=True)
    return jnp.floor(jnp.log2(jnp.maximum(top, 1e-30)))


LEVEL = 3.3


def encode(value, exponent):
    size = jnp.abs(value) * jnp.exp2(7.0 - exponent)
    binade = jnp.floor(jnp.log2(jnp.maximum(size, 1.0)))
    place = LEVEL * (binade + size * jnp.exp2(-binade))
    whole = jnp.floor(place)
    code = jnp.exp2(whole - 14.0) * (1.0 + (place - whole))
    return jnp.where(value < 0, -code, code)


def decode(code, exponent):
    size = jnp.abs(code)
    whole = jnp.floor(jnp.log2(jnp.maximum(size, 2.0**-14)))
    place = (whole + 13.0 + size * jnp.exp2(-whole)) * (1.0 / LEVEL)
    binade = jnp.maximum(jnp.floor(place) - 1.0, 0.0)
    value = (place - binade) * jnp.exp2(binade + exponent - 7.0)
    return jnp.where(code < 0, -value, value)


def pack_rows(tile, out):
    exponent = exponent_of(tile)
    tail = jnp.broadcast_to(exponent, (8, 128))
    sent = tile * jnp.exp2(14.0 - exponent)
    for x in range(4):
        for c in range(2):
            first = x * 128 + c * 64
            groups = [sent[first + i * 8 : first + (i + 1) * 8] for i in range(8)]
            out[x, c] = jnp.concatenate(groups + [tail], axis=1)


def summed_rows(parts):
    groups = [None] * 8
    for part in parts:
        scale = jnp.exp2(part[:, 4096:] - 14.0)
        scale = jnp.concatenate([scale] * 4, axis=1)
        for i in range(8):
            group = part[:, i * 512 : (i + 1) * 512] * scale
            groups[i] = group if groups[i] is None else groups[i] + group
    return jnp.concatenate(groups, axis=0)


def pack_blocks(tile, out):
    exponent = exponent_of(tile)
    tail = jnp.broadcast_to(exponent, (8, 128))
    sent = tile * jnp.exp2(14.0 - exponent)
    for x in range(4):
        for c in range(2):
            for y in range(4):
                first = x * 128 + c * 64 + y * 16
                top, bottom = sent[first : first + 8], sent[first + 8 : first + 16]
                out[y, x, c] = jnp.concatenate([top, bottom, tail], axis=1)


def unpack(sent):
    scale = jnp.exp2(sent[:, 1024:] - 14.0)
    scale = jnp.concatenate([scale] * 4, axis=1)
    return sent[:, :512] * scale, sent[:, 512:1024] * scale


def summed_blocks(parts):
    top, bottom = unpack(parts[0])
    for part in parts[1:]:
        more_top, more_bottom = unpack(part)
        top, bottom = top + more_top, bottom + more_bottom
    return jnp.concatenate([top, bottom], axis=0)


def tile_zero_kernel(prior, raw, out, total):
    step = pl.program_id(0)
    part = lax.dot_general(prior[...], raw[...], NT, preferred_element_type=F32)

    @pl.when(step == 0)
    def _():
        total[...] = part

    @pl.when(step > 0)
    def _():
        total[...] += part

    @pl.when(step == STEPS - 1)
    def _():
        pack_rows(total[...], out)


def tile_one_kernel(prior, raw_next, prior_last, raw, out):
    def form(left, right):
        pack_blocks(lax.dot_general(left[...], right[...], NT, preferred_element_type=F32), out)

    core = lax.axis_index("core")
    pl.when(core == 0)(lambda: form(prior, raw_next))
    pl.when(core == 1)(lambda: form(prior_last, raw))


def add_kernel(parts, out):
    out[...] = summed_rows([parts[x, c] for x in range(4) for c in range(2)])


def plane_prefix_kernel(zero, one, out):
    zeros, ones, late = [], [], None
    for lag in range(4):
        zeros.append(zero[lag] if lag == 0 else zeros[-1] + zero[lag])
        here, after = (summed_blocks([one[lag, x, c] for x in range(4)]) for c in range(2))
        if lag == 0:
            late, total = after, here + after
        else:
            ones.append(total + after)
            total = total + here + after
    ones.append(total)
    first = 0
    for i, parts in enumerate((zeros, ones, [late])):
        value = jnp.concatenate(parts, axis=0)
        exponent = exponent_of(value)
        value = encode(value, exponent)
        height = value.shape[0]
        for zl in range(4):
            out[zl, first : first + height] = value[:, zl * 128 : (zl + 1) * 128]
            out[zl, 144 + i * 8 : 152 + i * 8] = jnp.broadcast_to(exponent, (8, 128))
        first += height


def block_prefix_kernel(planes, local, total):
    def read(zl, i, first):
        exponent = planes[zl, 144 + i * 8 : 152 + i * 8]
        exponent = jnp.concatenate([exponent, exponent], axis=0)
        return decode(planes[zl, first : first + 16], exponent)

    zero, one = jnp.zeros((16, 128), F32), jnp.zeros((16, 128), F32)
    lates = [read(zl, 2, 128) for zl in range(4)]
    for zl in range(4):
        for lag in range(4):
            here_zero = zero + read(zl, 0, lag * 16)
            here_one = one + read(zl, 1, 64 + lag * 16)
            local[zl * 4 + lag, 0:16] = here_zero
            local[zl * 4 + lag, 16:32] = here_one + lates[zl + 1] if lag == 3 and zl < 3 else here_one
        zero, one = here_zero, here_one
    for i in range(4):
        total[i, 0:16] = zero
        total[i, 16:32] = one
        total[i, 32:48] = lates[0]


def finish_kernel(local, total, out):
    place = lax.axis_index("zh")
    earlier, late = jnp.zeros((32, 128), F32), jnp.zeros((16, 128), F32)
    for z in range(4):
        earlier = earlier + jnp.where(z < place, total[z, 0:32], 0.0)
        late = late + jnp.where(z == place + 1, total[z, 32:48], 0.0)
    for i in range(16):
        out[i] = local[i] + earlier
    out[15, 16:32] = local[15, 16:32] + earlier[16:32] + late


def split_kernel(rows, zero, one):
    for zl in range(4):
        for y in range(4):
            here, there = slice(y * 16, (y + 1) * 16), slice(zl * 128, (zl + 1) * 128)
            zero[0, here, there] = rows[zl * 4 + y, 0:16]
            one[0, here, there] = rows[zl * 4 + y, 16:32]


def exchange(value, axes):
    return lax.all_to_all(value, axes, 0, 0, tiled=True)


def exchange_short(value, axes):
    return exchange(value.astype(F16), axes).astype(F32)


def body(prior_rows, raw_rows):
    prior, raw = prior_rows[0], raw_rows[0]
    device = np.arange(512).reshape(64, 4, 2)
    down = [(int(device[l + 1, x, 0]), int(device[l, x, 0])) for l in range(63) for x in range(4)]
    up = [(int(device[l, x, 1]), int(device[l + 1, x, 1])) for l in range(63) for x in range(4)]
    raw_next = lax.ppermute(raw, LAG + PAR, down)
    prior_last = lax.ppermute(prior, LAG + PAR, up)

    piece = pl.BlockSpec((512, 2048 // STEPS), lambda step: (0, step))
    zero = pl.pallas_call(
        tile_zero_kernel,
        out_shape=shape(4, 2, 8, 4224),
        grid=(STEPS,),
        in_specs=[piece, piece],
        out_specs=VMEM,
        scratch_shapes=[pltpu.VMEM((512, 512), F32)],
        compiler_params=pltpu.CompilerParams(vmem_limit_bytes=8 * 2**20),
    )(far(prior), far(raw))
    zero = exchange_short(zero.reshape(8, 8, 4224), PAR).reshape(4, 2, 8, 4224)
    zero = exchange(call(add_kernel, shape(64, 512), zero).reshape(4, 16, 512), "y")

    raw_next, prior_last, zero = lax.optimization_barrier((raw_next, prior_last, zero))
    one = call(tile_one_kernel, shape(4, 4, 2, 8, 1152), prior, raw_next, prior_last, raw)
    one = exchange_short(one.reshape(32, 8, 1152), ("y", "x", "core")).reshape(4, 4, 2, 8, 1152)

    planes = exchange_short(call(plane_prefix_kernel, shape(4, 168, 128), zero, one), "zl")
    local, total = call(block_prefix_kernel, (shape(16, 32, 128), shape(4, 48, 128)), planes)
    rows = call(finish_kernel, shape(16, 32, 128), local, exchange(total, "zh"))
    return tuple(call(split_kernel, (result(1, 64, 512), result(1, 64, 512)), exchange(rows, ("zl", "y"))))


def solution(mesh):
    chips = Mesh(mesh.devices.reshape(4, 4, 4, 4, 2), LAG + PAR)
    in_specs = (P(LAG, None, PAR), P(LAG, None, PAR))
    out_specs = (P(LAG, PAR, None), P(LAG, PAR, None))
    return jax.shard_map(body, mesh=chips, in_specs=in_specs, out_specs=out_specs, check_vma=False)
```

```python
import jax
import jax.numpy as jnp
import numpy as np
from jax import lax
from jax.experimental import pallas as pl
from jax.experimental.pallas import tpu as pltpu
from jax.sharding import Mesh, PartitionSpec as P


F32 = jnp.float32
F16 = jnp.float16
NT = (((1,), (1,)), ((), ()))
LAG = ("zh", "zl", "y")
PAR = ("x", "core")
VMEM = pl.BlockSpec(memory_space=pltpu.VMEM)
STEPS = 4


def near(value):
    return pltpu.with_memory_space_constraint(value, pltpu.VMEM)


def far(value):
    return pltpu.with_memory_space_constraint(value, pltpu.HBM)


def call(kernel, out_shape, *args):
    return pl.pallas_call(
        kernel,
        out_shape=out_shape,
        in_specs=[VMEM] * len(args),
        out_specs=jax.tree.map(lambda _: VMEM, out_shape),
        compiler_params=pltpu.CompilerParams(vmem_limit_bytes=6 * 2**20),
    )(*[near(arg) for arg in args])


def shape(*dims):
    return pltpu.VMEM(dims, F32)


def result(*dims):
    return jax.ShapeDtypeStruct(dims, F32)


def exponent_of(value):
    top = jnp.max(jnp.max(jnp.abs(value), axis=0, keepdims=True), axis=1, keepdims=True)
    return jnp.floor(jnp.log2(jnp.maximum(top, 1e-30)))


LEVEL = 3.3


def encode(value, exponent):
    size = jnp.abs(value) * jnp.exp2(7.0 - exponent)
    binade = jnp.floor(jnp.log2(jnp.maximum(size, 1.0)))
    place = LEVEL * (binade + size * jnp.exp2(-binade))
    whole = jnp.floor(place)
    code = jnp.exp2(whole - 14.0) * (1.0 + (place - whole))
    return jnp.where(value < 0, -code, code)


def decode(code, exponent):
    size = jnp.abs(code)
    whole = jnp.floor(jnp.log2(jnp.maximum(size, 2.0**-14)))
    place = (whole + 13.0 + size * jnp.exp2(-whole)) * (1.0 / LEVEL)
    binade = jnp.maximum(jnp.floor(place) - 1.0, 0.0)
    value = (place - binade) * jnp.exp2(binade + exponent - 7.0)
    return jnp.where(code < 0, -value, value)


def pack_rows(tile, out):
    exponent = exponent_of(tile)
    tail = jnp.broadcast_to(exponent, (8, 128))
    sent = tile * jnp.exp2(14.0 - exponent)
    for x in range(4):
        for c in range(2):
            first = x * 128 + c * 64
            groups = [sent[first + i * 8 : first + (i + 1) * 8] for i in range(8)]
            out[x, c] = jnp.concatenate(groups + [tail], axis=1)


def summed_rows(parts):
    groups = [None] * 8
    for part in parts:
        scale = jnp.exp2(part[:, 4096:] - 14.0)
        scale = jnp.concatenate([scale] * 4, axis=1)
        for i in range(8):
            group = part[:, i * 512 : (i + 1) * 512] * scale
            groups[i] = group if groups[i] is None else groups[i] + group
    return jnp.concatenate(groups, axis=0)


def pack_blocks(tile, out):
    exponent = exponent_of(tile)
    tail = jnp.broadcast_to(exponent, (8, 128))
    sent = tile * jnp.exp2(14.0 - exponent)
    for x in range(4):
        for c in range(2):
            for y in range(4):
                first = x * 128 + c * 64 + y * 16
                top, bottom = sent[first : first + 8], sent[first + 8 : first + 16]
                out[y, x, c] = jnp.concatenate([top, bottom, tail], axis=1)


def unpack(sent):
    scale = jnp.exp2(sent[:, 1024:] - 14.0)
    scale = jnp.concatenate([scale] * 4, axis=1)
    return sent[:, :512] * scale, sent[:, 512:1024] * scale


def summed_blocks(parts):
    top, bottom = unpack(parts[0])
    for part in parts[1:]:
        more_top, more_bottom = unpack(part)
        top, bottom = top + more_top, bottom + more_bottom
    return jnp.concatenate([top, bottom], axis=0)


def tile_zero_kernel(prior, raw, out, total):
    step = pl.program_id(0)
    part = lax.dot_general(prior[...], raw[...], NT, preferred_element_type=F32)

    @pl.when(step == 0)
    def _():
        total[...] = part

    @pl.when(step > 0)
    def _():
        total[...] += part

    @pl.when(step == STEPS - 1)
    def _():
        pack_rows(total[...], out)


def tile_one_kernel(prior, raw_next, prior_last, raw, out):
    def form(left, right):
        pack_blocks(lax.dot_general(left[...], right[...], NT, preferred_element_type=F32), out)

    core = lax.axis_index("core")
    pl.when(core == 0)(lambda: form(prior, raw_next))
    pl.when(core == 1)(lambda: form(prior_last, raw))


def add_kernel(parts, out):
    out[...] = summed_rows([parts[x, c] for x in range(4) for c in range(2)])


def plane_prefix_kernel(zero, one, out):
    zeros, ones, late = [], [], None
    for lag in range(4):
        zeros.append(zero[lag] if lag == 0 else zeros[-1] + zero[lag])
        here, after = (summed_blocks([one[lag, x, c] for x in range(4)]) for c in range(2))
        if lag == 0:
            late, total = after, here + after
        else:
            ones.append(total + after)
            total = total + here + after
    ones.append(total)
    first = 0
    for i, parts in enumerate((zeros, ones, [late])):
        value = jnp.concatenate(parts, axis=0)
        exponent = exponent_of(value)
        value = encode(value, exponent)
        height = value.shape[0]
        for zl in range(4):
            out[zl, first : first + height] = value[:, zl * 128 : (zl + 1) * 128]
            out[zl, 144 + i * 8 : 152 + i * 8] = jnp.broadcast_to(exponent, (8, 128))
        first += height


def block_prefix_kernel(planes, local, total, late):
    def read(zl, i, first):
        exponent = planes[zl, 144 + i * 8 : 152 + i * 8]
        exponent = jnp.concatenate([exponent, exponent], axis=0)
        return decode(planes[zl, first : first + 16], exponent)

    zero, one = jnp.zeros((16, 128), F32), jnp.zeros((16, 128), F32)
    lates = [read(zl, 2, 128) for zl in range(4)]
    for zl in range(4):
        for lag in range(4):
            here_zero = zero + read(zl, 0, lag * 16)
            here_one = one + read(zl, 1, 64 + lag * 16)
            local[zl * 4 + lag, 0:16] = here_zero
            local[zl * 4 + lag, 16:32] = here_one + lates[zl + 1] if lag == 3 and zl < 3 else here_one
        zero, one = here_zero, here_one
    total[0:16], total[16:32] = zero, one
    late[...] = lates[0]


def sum_kernel(left, right, out):
    out[...] = left[...] + right[...]


def finish_kernel(local, first, second, third, late, out):
    earlier = first[...] + second[...] + third[...]
    for i in range(16):
        out[i] = local[i] + earlier
    out[15, 16:32] = local[15, 16:32] + earlier[16:32] + late[...]


def split_kernel(rows, zero, one):
    for zl in range(4):
        for y in range(4):
            here, there = slice(y * 16, (y + 1) * 16), slice(zl * 128, (zl + 1) * 128)
            zero[0, here, there] = rows[zl * 4 + y, 0:16]
            one[0, here, there] = rows[zl * 4 + y, 16:32]


def exchange(value, axes):
    return lax.all_to_all(value, axes, 0, 0, tiled=True)


def exchange_short(value, axes):
    return exchange(value.astype(F16), axes).astype(F32)


def body(prior_rows, raw_rows):
    prior, raw = prior_rows[0], raw_rows[0]
    device = np.arange(512).reshape(64, 4, 2)
    down = [(int(device[l + 1, x, 0]), int(device[l, x, 0])) for l in range(63) for x in range(4)]
    up = [(int(device[l, x, 1]), int(device[l + 1, x, 1])) for l in range(63) for x in range(4)]
    raw_next = lax.ppermute(raw, LAG + PAR, down)
    prior_last = lax.ppermute(prior, LAG + PAR, up)

    piece = pl.BlockSpec((512, 2048 // STEPS), lambda step: (0, step))
    zero = pl.pallas_call(
        tile_zero_kernel,
        out_shape=shape(4, 2, 8, 4224),
        grid=(STEPS,),
        in_specs=[piece, piece],
        out_specs=VMEM,
        scratch_shapes=[pltpu.VMEM((512, 512), F32)],
        compiler_params=pltpu.CompilerParams(vmem_limit_bytes=8 * 2**20),
    )(far(prior), far(raw))
    zero = exchange_short(zero.reshape(8, 8, 4224), PAR).reshape(4, 2, 8, 4224)
    zero = exchange(call(add_kernel, shape(64, 512), zero).reshape(4, 16, 512), "y")

    raw_next, prior_last, zero = lax.optimization_barrier((raw_next, prior_last, zero))
    one = call(tile_one_kernel, shape(4, 4, 2, 8, 1152), prior, raw_next, prior_last, raw)
    one = exchange_short(one.reshape(32, 8, 1152), ("y", "x", "core")).reshape(4, 4, 2, 8, 1152)

    planes = exchange_short(call(plane_prefix_kernel, shape(4, 168, 128), zero, one), "zl")
    shapes = shape(16, 32, 128), shape(32, 128), shape(16, 128)
    local, total, late = call(block_prefix_kernel, shapes, planes)
    late = lax.ppermute(late, "zh", [(1, 0), (2, 1), (3, 2)])
    first = lax.ppermute(total, "zh", [(0, 1)])
    total = call(sum_kernel, shape(32, 128), total, first)
    second = lax.ppermute(total, "zh", [(1, 2)])
    total = call(sum_kernel, shape(32, 128), total, second)
    third = lax.ppermute(total, "zh", [(2, 3)])
    rows = call(finish_kernel, shape(16, 32, 128), local, first, second, third, late)
    return tuple(call(split_kernel, (result(1, 64, 512), result(1, 64, 512)), exchange(rows, ("zl", "y"))))


def solution(mesh):
    chips = Mesh(mesh.devices.reshape(4, 4, 4, 4, 2), LAG + PAR)
    in_specs = (P(LAG, None, PAR), P(LAG, None, PAR))
    out_specs = (P(LAG, PAR, None), P(LAG, PAR, None))
    return jax.shard_map(body, mesh=chips, in_specs=in_specs, out_specs=out_specs, check_vma=False)
```

```python
import jax
import jax.numpy as jnp
import numpy as np
from jax import lax
from jax.experimental import pallas as pl
from jax.experimental.pallas import tpu as pltpu
from jax.sharding import Mesh, PartitionSpec as P


F32 = jnp.float32
F16 = jnp.float16
NT = (((1,), (1,)), ((), ()))
LAG = ("zh", "zl", "y")
PAR = ("x", "core")
VMEM = pl.BlockSpec(memory_space=pltpu.VMEM)
STEPS = 4


def near(value):
    return pltpu.with_memory_space_constraint(value, pltpu.VMEM)


def far(value):
    return pltpu.with_memory_space_constraint(value, pltpu.HBM)


def call(kernel, out_shape, *args):
    return pl.pallas_call(
        kernel,
        out_shape=out_shape,
        in_specs=[VMEM] * len(args),
        out_specs=jax.tree.map(lambda _: VMEM, out_shape),
        compiler_params=pltpu.CompilerParams(vmem_limit_bytes=6 * 2**20),
    )(*[near(arg) for arg in args])


def shape(*dims):
    return pltpu.VMEM(dims, F32)


def result(*dims):
    return jax.ShapeDtypeStruct(dims, F32)


def exponent_of(value):
    top = jnp.max(jnp.max(jnp.abs(value), axis=0, keepdims=True), axis=1, keepdims=True)
    return jnp.floor(jnp.log2(jnp.maximum(top, 1e-30)))


LEVEL = 3.3


def encode(value, exponent):
    size = jnp.abs(value) * jnp.exp2(7.0 - exponent)
    binade = jnp.floor(jnp.log2(jnp.maximum(size, 1.0)))
    place = LEVEL * (binade + size * jnp.exp2(-binade))
    whole = jnp.floor(place)
    code = jnp.exp2(whole - 14.0) * (1.0 + (place - whole))
    return jnp.where(value < 0, -code, code)


def decode(code, exponent):
    size = jnp.abs(code)
    whole = jnp.floor(jnp.log2(jnp.maximum(size, 2.0**-14)))
    place = (whole + 13.0 + size * jnp.exp2(-whole)) * (1.0 / LEVEL)
    binade = jnp.maximum(jnp.floor(place) - 1.0, 0.0)
    value = (place - binade) * jnp.exp2(binade + exponent - 7.0)
    return jnp.where(code < 0, -value, value)


def pack_rows(tile, out):
    exponent = exponent_of(tile)
    tail = jnp.broadcast_to(exponent, (8, 128))
    sent = tile * jnp.exp2(14.0 - exponent)
    for x in range(4):
        for c in range(2):
            first = x * 128 + c * 64
            groups = [sent[first + i * 8 : first + (i + 1) * 8] for i in range(8)]
            out[x, c] = jnp.concatenate(groups + [tail], axis=1)


def summed_rows(parts):
    groups = [None] * 8
    for part in parts:
        scale = jnp.exp2(part[:, 4096:] - 14.0)
        scale = jnp.concatenate([scale] * 4, axis=1)
        for i in range(8):
            group = part[:, i * 512 : (i + 1) * 512] * scale
            groups[i] = group if groups[i] is None else groups[i] + group
    return jnp.concatenate(groups, axis=0)


def pack_blocks(tile, out):
    exponent = exponent_of(tile)
    tail = jnp.broadcast_to(exponent, (8, 128))
    sent = tile * jnp.exp2(14.0 - exponent)
    for x in range(4):
        for c in range(2):
            for y in range(4):
                first = x * 128 + c * 64 + y * 16
                top, bottom = sent[first : first + 8], sent[first + 8 : first + 16]
                out[y, x, c] = jnp.concatenate([top, bottom, tail], axis=1)


def unpack(sent):
    scale = jnp.exp2(sent[:, 1024:] - 14.0)
    scale = jnp.concatenate([scale] * 4, axis=1)
    return sent[:, :512] * scale, sent[:, 512:1024] * scale


def summed_blocks(parts):
    top, bottom = unpack(parts[0])
    for part in parts[1:]:
        more_top, more_bottom = unpack(part)
        top, bottom = top + more_top, bottom + more_bottom
    return jnp.concatenate([top, bottom], axis=0)


def tile_zero_kernel(prior, raw, out, total):
    step = pl.program_id(0)
    part = lax.dot_general(prior[...], raw[...], NT, preferred_element_type=F32)

    @pl.when(step == 0)
    def _():
        total[...] = part

    @pl.when(step > 0)
    def _():
        total[...] += part

    @pl.when(step == STEPS - 1)
    def _():
        pack_rows(total[...], out)


def tile_one_kernel(prior, raw_next, prior_last, raw, out):
    def form(left, right):
        pack_blocks(lax.dot_general(left[...], right[...], NT, preferred_element_type=F32), out)

    core = lax.axis_index("core")
    pl.when(core == 0)(lambda: form(prior, raw_next))
    pl.when(core == 1)(lambda: form(prior_last, raw))


def add_kernel(parts, out):
    out[...] = summed_rows([parts[x, c] for x in range(4) for c in range(2)])


def plane_prefix_kernel(zero, one, out):
    zeros, ones, late = [], [], None
    for lag in range(4):
        zeros.append(zero[lag] if lag == 0 else zeros[-1] + zero[lag])
        here, after = (summed_blocks([one[lag, x, c] for x in range(4)]) for c in range(2))
        if lag == 0:
            late, total = after, here + after
        else:
            ones.append(total + after)
            total = total + here + after
    ones.append(total)
    first = 0
    for i, parts in enumerate((zeros, ones, [late])):
        value = jnp.concatenate(parts, axis=0)
        exponent = exponent_of(value)
        value = encode(value, exponent)
        height = value.shape[0]
        for zl in range(4):
            out[zl, first : first + height] = value[:, zl * 128 : (zl + 1) * 128]
            out[zl, 144 + i * 8 : 152 + i * 8] = jnp.broadcast_to(exponent, (8, 128))
        first += height


def block_prefix_kernel(planes, local, total):
    def read(zl, i, first):
        exponent = planes[zl, 144 + i * 8 : 152 + i * 8]
        exponent = jnp.concatenate([exponent, exponent], axis=0)
        return decode(planes[zl, first : first + 16], exponent)

    zero, one = jnp.zeros((16, 128), F32), jnp.zeros((16, 128), F32)
    lates = [read(zl, 2, 128) for zl in range(4)]
    for zl in range(4):
        for lag in range(4):
            here_zero = zero + read(zl, 0, lag * 16)
            here_one = one + read(zl, 1, 64 + lag * 16)
            local[zl * 4 + lag, 0:16] = here_zero
            local[zl * 4 + lag, 16:32] = here_one + lates[zl + 1] if lag == 3 and zl < 3 else here_one
        zero, one = here_zero, here_one
    total[0:16], total[16:32], total[32:48] = zero, one, lates[0]


def sum_kernel(total, other, out):
    out[0:32] = total[0:32] + other[0:32]
    out[32:48] = total[32:48]


def finish_kernel(local, early, crossed, own, out):
    place = lax.axis_index("zh")

    def pick(chosen, ref, first, last):
        return jnp.where(chosen, ref[first:last], 0.0)

    earlier = pick(place == 1, early, 0, 32) + pick(place >= 2, crossed, 0, 32) + pick(place == 3, own, 0, 32)
    late = pick(place == 0, early, 32, 48) + pick(place == 1, crossed, 32, 48) + pick(place == 2, own, 32, 48)
    for i in range(16):
        out[i] = local[i] + earlier
    out[15, 16:32] = local[15, 16:32] + earlier[16:32] + late


def split_kernel(rows, zero, one):
    for zl in range(4):
        for y in range(4):
            here, there = slice(y * 16, (y + 1) * 16), slice(zl * 128, (zl + 1) * 128)
            zero[0, here, there] = rows[zl * 4 + y, 0:16]
            one[0, here, there] = rows[zl * 4 + y, 16:32]


def exchange(value, axes):
    return lax.all_to_all(value, axes, 0, 0, tiled=True)


def exchange_short(value, axes):
    return exchange(value.astype(F16), axes).astype(F32)


def body(prior_rows, raw_rows):
    prior, raw = prior_rows[0], raw_rows[0]
    device = np.arange(512).reshape(64, 4, 2)
    down = [(int(device[l + 1, x, 0]), int(device[l, x, 0])) for l in range(63) for x in range(4)]
    up = [(int(device[l, x, 1]), int(device[l + 1, x, 1])) for l in range(63) for x in range(4)]
    raw_next = lax.ppermute(raw, LAG + PAR, down)
    prior_last = lax.ppermute(prior, LAG + PAR, up)

    piece = pl.BlockSpec((512, 2048 // STEPS), lambda step: (0, step))
    zero = pl.pallas_call(
        tile_zero_kernel,
        out_shape=shape(4, 2, 8, 4224),
        grid=(STEPS,),
        in_specs=[piece, piece],
        out_specs=VMEM,
        scratch_shapes=[pltpu.VMEM((512, 512), F32)],
        compiler_params=pltpu.CompilerParams(vmem_limit_bytes=8 * 2**20),
    )(far(prior), far(raw))
    zero = exchange_short(zero.reshape(8, 8, 4224), PAR).reshape(4, 2, 8, 4224)
    zero = exchange(call(add_kernel, shape(64, 512), zero).reshape(4, 16, 512), "y")

    raw_next, prior_last, zero = lax.optimization_barrier((raw_next, prior_last, zero))
    one = call(tile_one_kernel, shape(4, 4, 2, 8, 1152), prior, raw_next, prior_last, raw)
    one = exchange_short(one.reshape(32, 8, 1152), ("y", "x", "core")).reshape(4, 4, 2, 8, 1152)

    planes = exchange_short(call(plane_prefix_kernel, shape(4, 168, 128), zero, one), "zl")
    local, total = call(block_prefix_kernel, (shape(16, 32, 128), shape(48, 128)), planes)
    early = lax.ppermute(total, "zh", [(0, 1), (1, 0)])
    both = call(sum_kernel, shape(48, 128), total, early)
    crossed = lax.ppermute(both, "zh", [(1, 2), (2, 1), (0, 3)])
    own = lax.ppermute(total, "zh", [(2, 3), (3, 2)])
    rows = call(finish_kernel, shape(16, 32, 128), local, early, crossed, own)
    return tuple(call(split_kernel, (result(1, 64, 512), result(1, 64, 512)), exchange(rows, ("zl", "y"))))


def solution(mesh):
    chips = Mesh(mesh.devices.reshape(4, 4, 4, 4, 2), LAG + PAR)
    in_specs = (P(LAG, None, PAR), P(LAG, None, PAR))
    out_specs = (P(LAG, PAR, None), P(LAG, PAR, None))
    return jax.shard_map(body, mesh=chips, in_specs=in_specs, out_specs=out_specs, check_vma=False)
```

```python
import jax
import jax.numpy as jnp
import numpy as np
from jax import lax
from jax.experimental import pallas as pl
from jax.experimental.pallas import tpu as pltpu
from jax.sharding import Mesh, PartitionSpec as P


F32 = jnp.float32
F16 = jnp.float16
NT = (((1,), (1,)), ((), ()))
LAG = ("zh", "zl", "y")
PAR = ("x", "core")
VMEM = pl.BlockSpec(memory_space=pltpu.VMEM)
STEPS = 4


def near(value):
    return pltpu.with_memory_space_constraint(value, pltpu.VMEM)


def far(value):
    return pltpu.with_memory_space_constraint(value, pltpu.HBM)


def call(kernel, out_shape, *args):
    return pl.pallas_call(
        kernel,
        out_shape=out_shape,
        in_specs=[VMEM] * len(args),
        out_specs=jax.tree.map(lambda _: VMEM, out_shape),
        compiler_params=pltpu.CompilerParams(vmem_limit_bytes=6 * 2**20),
    )(*[near(arg) for arg in args])


def shape(*dims):
    return pltpu.VMEM(dims, F32)


def result(*dims):
    return jax.ShapeDtypeStruct(dims, F32)


def exponent_of(value):
    top = jnp.max(jnp.max(jnp.abs(value), axis=0, keepdims=True), axis=1, keepdims=True)
    return jnp.floor(jnp.log2(jnp.maximum(top, 1e-30)))


LEVEL = 3.3


def encode(value, exponent):
    size = jnp.abs(value) * jnp.exp2(7.0 - exponent)
    binade = jnp.floor(jnp.log2(jnp.maximum(size, 1.0)))
    place = LEVEL * (binade + size * jnp.exp2(-binade))
    whole = jnp.floor(place)
    code = jnp.exp2(whole - 14.0) * (1.0 + (place - whole))
    return jnp.where(value < 0, -code, code)


def decode(code, exponent):
    size = jnp.abs(code)
    whole = jnp.floor(jnp.log2(jnp.maximum(size, 2.0**-14)))
    place = (whole + 13.0 + size * jnp.exp2(-whole)) * (1.0 / LEVEL)
    binade = jnp.maximum(jnp.floor(place) - 1.0, 0.0)
    value = (place - binade) * jnp.exp2(binade + exponent - 7.0)
    return jnp.where(code < 0, -value, value)


def pack_rows(tile, out):
    exponent = exponent_of(tile)
    tail = jnp.broadcast_to(exponent, (8, 128))
    sent = tile * jnp.exp2(14.0 - exponent)
    for x in range(4):
        for c in range(2):
            first = x * 128 + c * 64
            groups = [sent[first + i * 8 : first + (i + 1) * 8] for i in range(8)]
            out[x, c] = jnp.concatenate(groups + [tail], axis=1)


def summed_rows(parts):
    groups = [None] * 8
    for part in parts:
        scale = jnp.exp2(part[:, 4096:] - 14.0)
        scale = jnp.concatenate([scale] * 4, axis=1)
        for i in range(8):
            group = part[:, i * 512 : (i + 1) * 512] * scale
            groups[i] = group if groups[i] is None else groups[i] + group
    return jnp.concatenate(groups, axis=0)


def pack_blocks(tile, out):
    exponent = exponent_of(tile)
    tail = jnp.broadcast_to(exponent, (8, 128))
    sent = tile * jnp.exp2(14.0 - exponent)
    for x in range(4):
        for c in range(2):
            for y in range(4):
                first = x * 128 + c * 64 + y * 16
                top, bottom = sent[first : first + 8], sent[first + 8 : first + 16]
                out[y, x, c] = jnp.concatenate([top, bottom, tail], axis=1)


def unpack(sent):
    scale = jnp.exp2(sent[:, 1024:] - 14.0)
    scale = jnp.concatenate([scale] * 4, axis=1)
    return sent[:, :512] * scale, sent[:, 512:1024] * scale


def summed_blocks(parts):
    top, bottom = unpack(parts[0])
    for part in parts[1:]:
        more_top, more_bottom = unpack(part)
        top, bottom = top + more_top, bottom + more_bottom
    return jnp.concatenate([top, bottom], axis=0)


def tile_zero_kernel(prior, raw, out, total):
    step = pl.program_id(0)
    part = lax.dot_general(prior[...], raw[...], NT, preferred_element_type=F32)

    @pl.when(step == 0)
    def _():
        total[...] = part

    @pl.when(step > 0)
    def _():
        total[...] += part

    @pl.when(step == STEPS - 1)
    def _():
        pack_rows(total[...], out)


def tile_one_kernel(prior, raw_next, prior_last, raw, out):
    def form(left, right):
        pack_blocks(lax.dot_general(left[...], right[...], NT, preferred_element_type=F32), out)

    core = lax.axis_index("core")
    pl.when(core == 0)(lambda: form(prior, raw_next))
    pl.when(core == 1)(lambda: form(prior_last, raw))


def add_kernel(parts, out):
    out[...] = summed_rows([parts[x, c] for x in range(4) for c in range(2)])


def plane_prefix_kernel(zero, one, out):
    zeros, ones, late = [], [], None
    for lag in range(4):
        zeros.append(zero[lag] if lag == 0 else zeros[-1] + zero[lag])
        here, after = (summed_blocks([one[lag, x, c] for x in range(4)]) for c in range(2))
        if lag == 0:
            late, total = after, here + after
        else:
            ones.append(total + after)
            total = total + here + after
    ones.append(total)
    first = 0
    for i, parts in enumerate((zeros, ones, [late])):
        value = jnp.concatenate(parts, axis=0)
        exponent = exponent_of(value)
        value = encode(value, exponent)
        height = value.shape[0]
        for zl in range(4):
            out[zl, first : first + height] = value[:, zl * 128 : (zl + 1) * 128]
            out[zl, 144 + i * 8 : 152 + i * 8] = jnp.broadcast_to(exponent, (8, 128))
        first += height


def block_prefix_kernel(planes, local, total):
    def read(zl, i, first):
        exponent = planes[zl, 144 + i * 8 : 152 + i * 8]
        exponent = jnp.concatenate([exponent, exponent], axis=0)
        return decode(planes[zl, first : first + 16], exponent)

    zero, one = jnp.zeros((16, 128), F32), jnp.zeros((16, 128), F32)
    lates = [read(zl, 2, 128) for zl in range(4)]
    for zl in range(4):
        for lag in range(4):
            here_zero = zero + read(zl, 0, lag * 16)
            here_one = one + read(zl, 1, 64 + lag * 16)
            local[zl * 4 + lag, 0:16] = here_zero
            local[zl * 4 + lag, 16:32] = here_one + lates[zl + 1] if lag == 3 and zl < 3 else here_one
        zero, one = here_zero, here_one
    total[0:16], total[16:32], total[32:48] = zero, one, lates[0]


def sum_kernel(total, other, out):
    out[0:32] = total[0:32] + other[0:32]
    out[32:48] = total[32:48]


def finish_kernel(local, early, back, crossed, own, out):
    place = lax.axis_index("zh")

    def pick(chosen, ref, first, last):
        return jnp.where(chosen, ref[first:last], 0.0)

    earlier = pick(place == 1, early, 0, 32) + pick(place >= 2, crossed, 0, 32) + pick(place == 3, own, 0, 32)
    late = pick(place == 0, early, 32, 48) + pick(place == 1, back, 32, 48) + pick(place == 2, own, 32, 48)
    for i in range(16):
        out[i] = local[i] + earlier
    out[15, 16:32] = local[15, 16:32] + earlier[16:32] + late


def split_kernel(rows, zero, one):
    for zl in range(4):
        for y in range(4):
            here, there = slice(y * 16, (y + 1) * 16), slice(zl * 128, (zl + 1) * 128)
            zero[0, here, there] = rows[zl * 4 + y, 0:16]
            one[0, here, there] = rows[zl * 4 + y, 16:32]


def exchange(value, axes):
    return lax.all_to_all(value, axes, 0, 0, tiled=True)


def exchange_short(value, axes):
    return exchange(value.astype(F16), axes).astype(F32)


def body(prior_rows, raw_rows):
    prior, raw = prior_rows[0], raw_rows[0]
    device = np.arange(512).reshape(64, 4, 2)
    down = [(int(device[l + 1, x, 0]), int(device[l, x, 0])) for l in range(63) for x in range(4)]
    up = [(int(device[l, x, 1]), int(device[l + 1, x, 1])) for l in range(63) for x in range(4)]
    raw_next = lax.ppermute(raw, LAG + PAR, down)
    prior_last = lax.ppermute(prior, LAG + PAR, up)

    piece = pl.BlockSpec((512, 2048 // STEPS), lambda step: (0, step))
    zero = pl.pallas_call(
        tile_zero_kernel,
        out_shape=shape(4, 2, 8, 4224),
        grid=(STEPS,),
        in_specs=[piece, piece],
        out_specs=VMEM,
        scratch_shapes=[pltpu.VMEM((512, 512), F32)],
        compiler_params=pltpu.CompilerParams(vmem_limit_bytes=8 * 2**20),
    )(far(prior), far(raw))
    zero = exchange_short(zero.reshape(8, 8, 4224), PAR).reshape(4, 2, 8, 4224)
    zero = exchange(call(add_kernel, shape(64, 512), zero).reshape(4, 16, 512), "y")

    raw_next, prior_last, zero = lax.optimization_barrier((raw_next, prior_last, zero))
    one = call(tile_one_kernel, shape(4, 4, 2, 8, 1152), prior, raw_next, prior_last, raw)
    one = exchange_short(one.reshape(32, 8, 1152), ("y", "x", "core")).reshape(4, 4, 2, 8, 1152)

    planes = exchange_short(call(plane_prefix_kernel, shape(4, 168, 128), zero, one), "zl")
    local, total = call(block_prefix_kernel, (shape(16, 32, 128), shape(48, 128)), planes)
    early = lax.ppermute(total, "zh", [(0, 1), (1, 0)])
    back = lax.ppermute(total, "zh", [(2, 1)])
    both = call(sum_kernel, shape(48, 128), total, early)
    crossed = lax.ppermute(both, "zh", [(1, 2), (0, 3)])
    own = lax.ppermute(total, "zh", [(2, 3), (3, 2)])
    rows = call(finish_kernel, shape(16, 32, 128), local, early, back, crossed, own)
    return tuple(call(split_kernel, (result(1, 64, 512), result(1, 64, 512)), exchange(rows, ("zl", "y"))))


def solution(mesh):
    chips = Mesh(mesh.devices.reshape(4, 4, 4, 4, 2), LAG + PAR)
    in_specs = (P(LAG, None, PAR), P(LAG, None, PAR))
    out_specs = (P(LAG, PAR, None), P(LAG, PAR, None))
    return jax.shard_map(body, mesh=chips, in_specs=in_specs, out_specs=out_specs, check_vma=False)
```

```python
import jax
import jax.numpy as jnp
import numpy as np
from jax import lax
from jax.experimental import pallas as pl
from jax.experimental.pallas import tpu as pltpu
from jax.sharding import Mesh, PartitionSpec as P


F32 = jnp.float32
F16 = jnp.float16
NT = (((1,), (1,)), ((), ()))
LAG = ("zh", "zl", "y")
PAR = ("x", "core")
VMEM = pl.BlockSpec(memory_space=pltpu.VMEM)
STEPS = 4


def near(value):
    return pltpu.with_memory_space_constraint(value, pltpu.VMEM)


def far(value):
    return pltpu.with_memory_space_constraint(value, pltpu.HBM)


def call(kernel, out_shape, *args):
    return pl.pallas_call(
        kernel,
        out_shape=out_shape,
        in_specs=[VMEM] * len(args),
        out_specs=jax.tree.map(lambda _: VMEM, out_shape),
        compiler_params=pltpu.CompilerParams(vmem_limit_bytes=6 * 2**20),
    )(*[near(arg) for arg in args])


def shape(*dims):
    return pltpu.VMEM(dims, F32)


def result(*dims):
    return jax.ShapeDtypeStruct(dims, F32)


def exponent_of(value):
    top = jnp.max(jnp.max(jnp.abs(value), axis=0, keepdims=True), axis=1, keepdims=True)
    return jnp.floor(jnp.log2(jnp.maximum(top, 1e-30)))


LEVEL = 3.3


def encode(value, exponent):
    size = jnp.abs(value) * jnp.exp2(7.0 - exponent)
    binade = jnp.floor(jnp.log2(jnp.maximum(size, 1.0)))
    place = LEVEL * (binade + size * jnp.exp2(-binade))
    whole = jnp.floor(place)
    code = jnp.exp2(whole - 14.0) * (1.0 + (place - whole))
    return jnp.where(value < 0, -code, code)


def decode(code, exponent):
    size = jnp.abs(code)
    whole = jnp.floor(jnp.log2(jnp.maximum(size, 2.0**-14)))
    place = (whole + 13.0 + size * jnp.exp2(-whole)) * (1.0 / LEVEL)
    binade = jnp.maximum(jnp.floor(place) - 1.0, 0.0)
    value = (place - binade) * jnp.exp2(binade + exponent - 7.0)
    return jnp.where(code < 0, -value, value)


def pack_rows(tile, out):
    exponent = exponent_of(tile)
    tail = jnp.broadcast_to(exponent, (8, 128))
    sent = tile * jnp.exp2(14.0 - exponent)
    for x in range(4):
        for c in range(2):
            first = x * 128 + c * 64
            groups = [sent[first + i * 8 : first + (i + 1) * 8] for i in range(8)]
            out[x, c] = jnp.concatenate(groups + [tail], axis=1)


def summed_rows(parts):
    groups = [None] * 8
    for part in parts:
        scale = jnp.exp2(part[:, 4096:] - 14.0)
        scale = jnp.concatenate([scale] * 4, axis=1)
        for i in range(8):
            group = part[:, i * 512 : (i + 1) * 512] * scale
            groups[i] = group if groups[i] is None else groups[i] + group
    return jnp.concatenate(groups, axis=0)


def pack_blocks(tile, out):
    exponent = exponent_of(tile)
    tail = jnp.broadcast_to(exponent, (8, 128))
    sent = tile * jnp.exp2(14.0 - exponent)
    for x in range(4):
        for c in range(2):
            for y in range(4):
                first = x * 128 + c * 64 + y * 16
                top, bottom = sent[first : first + 8], sent[first + 8 : first + 16]
                out[y, x, c] = jnp.concatenate([top, bottom, tail], axis=1)


def unpack(sent):
    scale = jnp.exp2(sent[:, 1024:] - 14.0)
    scale = jnp.concatenate([scale] * 4, axis=1)
    return sent[:, :512] * scale, sent[:, 512:1024] * scale


def summed_blocks(parts):
    top, bottom = unpack(parts[0])
    for part in parts[1:]:
        more_top, more_bottom = unpack(part)
        top, bottom = top + more_top, bottom + more_bottom
    return jnp.concatenate([top, bottom], axis=0)


def tile_zero_kernel(prior, raw, out, prior_near, raw_near, total, sems):
    width = 2048 // STEPS
    copies = []
    for step in range(STEPS):
        group = []
        for i in range(4):
            source, target = (prior, prior_near) if i < 2 else (raw, raw_near)
            piece = (pl.ds(i % 2 * 256, 256), pl.ds(step * width, width))
            group.append(pltpu.make_async_copy(source.at[piece], target.at[piece], sems.at[step * 4 + i]))
        copies.append(group)
    for group in copies:
        for copy in group:
            copy.start()
    for step, group in enumerate(copies):
        for copy in group:
            copy.wait()
        columns = slice(step * width, (step + 1) * width)
        part = lax.dot_general(prior_near[:, columns], raw_near[:, columns], NT, preferred_element_type=F32)
        if step == 0:
            total[...] = part
        else:
            total[...] += part
    pack_rows(total[...], out)


def tile_one_kernel(prior, raw_next, prior_last, raw, out):
    def form(left, right):
        pack_blocks(lax.dot_general(left[...], right[...], NT, preferred_element_type=F32), out)

    core = lax.axis_index("core")
    pl.when(core == 0)(lambda: form(prior, raw_next))
    pl.when(core == 1)(lambda: form(prior_last, raw))


def add_kernel(parts, out):
    out[...] = summed_rows([parts[x, c] for x in range(4) for c in range(2)])


def plane_prefix_kernel(zero, one, out):
    zeros, ones, late = [], [], None
    for lag in range(4):
        zeros.append(zero[lag] if lag == 0 else zeros[-1] + zero[lag])
        here, after = (summed_blocks([one[lag, x, c] for x in range(4)]) for c in range(2))
        if lag == 0:
            late, total = after, here + after
        else:
            ones.append(total + after)
            total = total + here + after
    ones.append(total)
    first = 0
    for i, parts in enumerate((zeros, ones, [late])):
        value = jnp.concatenate(parts, axis=0)
        exponent = exponent_of(value)
        value = encode(value, exponent)
        height = value.shape[0]
        for zl in range(4):
            out[zl, first : first + height] = value[:, zl * 128 : (zl + 1) * 128]
            out[zl, 144 + i * 8 : 152 + i * 8] = jnp.broadcast_to(exponent, (8, 128))
        first += height


def block_prefix_kernel(planes, local, total):
    def read(zl, i, first):
        exponent = planes[zl, 144 + i * 8 : 152 + i * 8]
        exponent = jnp.concatenate([exponent, exponent], axis=0)
        return decode(planes[zl, first : first + 16], exponent)

    zero, one = jnp.zeros((16, 128), F32), jnp.zeros((16, 128), F32)
    lates = [read(zl, 2, 128) for zl in range(4)]
    for zl in range(4):
        for lag in range(4):
            here_zero = zero + read(zl, 0, lag * 16)
            here_one = one + read(zl, 1, 64 + lag * 16)
            local[zl * 4 + lag, 0:16] = here_zero
            local[zl * 4 + lag, 16:32] = here_one + lates[zl + 1] if lag == 3 and zl < 3 else here_one
        zero, one = here_zero, here_one
    total[0:16], total[16:32], total[32:48] = zero, one, lates[0]


def sum_kernel(total, other, out):
    out[0:32] = total[0:32] + other[0:32]
    out[32:48] = total[32:48]


def finish_kernel(local, early, back, crossed, own, out):
    place = lax.axis_index("zh")

    def pick(chosen, ref, first, last):
        return jnp.where(chosen, ref[first:last], 0.0)

    earlier = pick(place == 1, early, 0, 32) + pick(place >= 2, crossed, 0, 32) + pick(place == 3, own, 0, 32)
    late = pick(place == 0, early, 32, 48) + pick(place == 1, back, 32, 48) + pick(place == 2, own, 32, 48)
    for i in range(16):
        out[i] = local[i] + earlier
    out[15, 16:32] = local[15, 16:32] + earlier[16:32] + late


def split_kernel(rows, zero, one):
    for zl in range(4):
        for y in range(4):
            here, there = slice(y * 16, (y + 1) * 16), slice(zl * 128, (zl + 1) * 128)
            zero[0, here, there] = rows[zl * 4 + y, 0:16]
            one[0, here, there] = rows[zl * 4 + y, 16:32]


def exchange(value, axes):
    return lax.all_to_all(value, axes, 0, 0, tiled=True)


def exchange_short(value, axes):
    return exchange(value.astype(F16), axes).astype(F32)


def body(prior_rows, raw_rows):
    prior, raw = prior_rows[0], raw_rows[0]
    device = np.arange(512).reshape(64, 4, 2)
    down = [(int(device[l + 1, x, 0]), int(device[l, x, 0])) for l in range(63) for x in range(4)]
    up = [(int(device[l, x, 1]), int(device[l + 1, x, 1])) for l in range(63) for x in range(4)]
    raw_next = lax.ppermute(raw, LAG + PAR, down)
    prior_last = lax.ppermute(prior, LAG + PAR, up)

    full = pltpu.VMEM((512, 2048), jnp.bfloat16)
    zero, prior, raw = pl.pallas_call(
        tile_zero_kernel,
        out_shape=(shape(4, 2, 8, 4224), full, full),
        in_specs=[pl.BlockSpec(memory_space=pltpu.HBM)] * 2,
        out_specs=(VMEM,) * 3,
        scratch_shapes=[pltpu.VMEM((512, 512), F32), pltpu.SemaphoreType.DMA((STEPS * 4,))],
        compiler_params=pltpu.CompilerParams(vmem_limit_bytes=8 * 2**20),
    )(far(prior), far(raw))
    zero = exchange_short(zero.reshape(8, 8, 4224), PAR).reshape(4, 2, 8, 4224)
    zero = exchange(call(add_kernel, shape(64, 512), zero).reshape(4, 16, 512), "y")

    raw_next, prior_last, zero = lax.optimization_barrier((raw_next, prior_last, zero))
    one = call(tile_one_kernel, shape(4, 4, 2, 8, 1152), prior, raw_next, prior_last, raw)
    one = exchange_short(one.reshape(32, 8, 1152), ("y", "x", "core")).reshape(4, 4, 2, 8, 1152)

    planes = exchange_short(call(plane_prefix_kernel, shape(4, 168, 128), zero, one), "zl")
    local, total = call(block_prefix_kernel, (shape(16, 32, 128), shape(48, 128)), planes)
    early = lax.ppermute(total, "zh", [(0, 1), (1, 0)])
    back = lax.ppermute(total, "zh", [(2, 1)])
    both = call(sum_kernel, shape(48, 128), total, early)
    crossed = lax.ppermute(both, "zh", [(1, 2), (0, 3)])
    own = lax.ppermute(total, "zh", [(2, 3), (3, 2)])
    rows = call(finish_kernel, shape(16, 32, 128), local, early, back, crossed, own)
    return tuple(call(split_kernel, (result(1, 64, 512), result(1, 64, 512)), exchange(rows, ("zl", "y"))))


def solution(mesh):
    chips = Mesh(mesh.devices.reshape(4, 4, 4, 4, 2), LAG + PAR)
    in_specs = (P(LAG, None, PAR), P(LAG, None, PAR))
    out_specs = (P(LAG, PAR, None), P(LAG, PAR, None))
    return jax.shard_map(body, mesh=chips, in_specs=in_specs, out_specs=out_specs, check_vma=False)
```

```python
import jax
import jax.numpy as jnp
import numpy as np
from jax import lax
from jax.experimental import pallas as pl
from jax.experimental.pallas import tpu as pltpu
from jax.sharding import Mesh, PartitionSpec as P


F32 = jnp.float32
F16 = jnp.float16
NT = (((1,), (1,)), ((), ()))
LAG = ("zh", "zl", "y")
PAR = ("x", "core")
VMEM = pl.BlockSpec(memory_space=pltpu.VMEM)
STEPS = 4


def near(value):
    return pltpu.with_memory_space_constraint(value, pltpu.VMEM)


def far(value):
    return pltpu.with_memory_space_constraint(value, pltpu.HBM)


def call(kernel, out_shape, *args, scratch=()):
    return pl.pallas_call(
        kernel,
        out_shape=out_shape,
        scratch_shapes=scratch,
        in_specs=[VMEM] * len(args),
        out_specs=jax.tree.map(lambda _: VMEM, out_shape),
        compiler_params=pltpu.CompilerParams(vmem_limit_bytes=6 * 2**20),
    )(*[near(arg) for arg in args])


def shape(*dims):
    return pltpu.VMEM(dims, F32)


def result(*dims):
    return jax.ShapeDtypeStruct(dims, F32)


def exponent_of(value):
    top = jnp.max(jnp.max(jnp.abs(value), axis=0, keepdims=True), axis=1, keepdims=True)
    return jnp.floor(jnp.log2(jnp.maximum(top, 1e-30)))


LEVEL = 3.3


def encode(value, exponent):
    size = jnp.abs(value) * jnp.exp2(7.0 - exponent)
    binade = jnp.floor(jnp.log2(jnp.maximum(size, 1.0)))
    place = LEVEL * (binade + size * jnp.exp2(-binade))
    whole = jnp.floor(place)
    code = jnp.exp2(whole - 14.0) * (1.0 + (place - whole))
    return jnp.where(value < 0, -code, code)


def decode(code, exponent):
    size = jnp.abs(code)
    whole = jnp.floor(jnp.log2(jnp.maximum(size, 2.0**-14)))
    place = (whole + 13.0 + size * jnp.exp2(-whole)) * (1.0 / LEVEL)
    binade = jnp.maximum(jnp.floor(place) - 1.0, 0.0)
    value = (place - binade) * jnp.exp2(binade + exponent - 7.0)
    return jnp.where(code < 0, -value, value)


def pack_rows(tile, out):
    exponent = exponent_of(tile)
    tail = jnp.broadcast_to(exponent, (8, 128))
    sent = tile * jnp.exp2(14.0 - exponent)
    for x in range(4):
        for c in range(2):
            first = x * 128 + c * 64
            groups = [sent[first + i * 8 : first + (i + 1) * 8] for i in range(8)]
            out[x, c] = jnp.concatenate(groups + [tail], axis=1)


def summed_rows(parts):
    groups = [None] * 8
    for part in parts:
        scale = jnp.exp2(part[:, 4096:] - 14.0)
        scale = jnp.concatenate([scale] * 4, axis=1)
        for i in range(8):
            group = part[:, i * 512 : (i + 1) * 512] * scale
            groups[i] = group if groups[i] is None else groups[i] + group
    return jnp.concatenate(groups, axis=0)


def pack_blocks(tile, out):
    exponent = exponent_of(tile)
    tail = jnp.broadcast_to(exponent, (8, 128))
    sent = tile * jnp.exp2(14.0 - exponent)
    for x in range(4):
        for c in range(2):
            for y in range(4):
                first = x * 128 + c * 64 + y * 16
                top, bottom = sent[first : first + 8], sent[first + 8 : first + 16]
                out[y, x, c] = jnp.concatenate([top, bottom, tail], axis=1)


def unpack(sent):
    scale = jnp.exp2(sent[:, 1024:] - 14.0)
    scale = jnp.concatenate([scale] * 4, axis=1)
    return sent[:, :512] * scale, sent[:, 512:1024] * scale


def summed_blocks(parts):
    top, bottom = unpack(parts[0])
    for part in parts[1:]:
        more_top, more_bottom = unpack(part)
        top, bottom = top + more_top, bottom + more_bottom
    return jnp.concatenate([top, bottom], axis=0)


def tile_zero_kernel(prior, raw, out, prior_near, raw_near, total, sems):
    width = 2048 // STEPS
    copies = []
    for step in range(STEPS):
        group = []
        for i in range(4):
            source, target = (prior, prior_near) if i < 2 else (raw, raw_near)
            piece = (pl.ds(i % 2 * 256, 256), pl.ds(step * width, width))
            group.append(pltpu.make_async_copy(source.at[piece], target.at[piece], sems.at[step * 4 + i]))
        copies.append(group)
    for group in copies:
        for copy in group:
            copy.start()
    for step, group in enumerate(copies):
        for copy in group:
            copy.wait()
        columns = slice(step * width, (step + 1) * width)
        part = lax.dot_general(prior_near[:, columns], raw_near[:, columns], NT, preferred_element_type=F32)
        if step == 0:
            total[...] = part
        else:
            total[...] += part
    pack_rows(total[...], out)


def tile_one_kernel(prior, raw_next, prior_last, raw, out):
    def form(left, right):
        pack_blocks(lax.dot_general(left[...], right[...], NT, preferred_element_type=F32), out)

    core = lax.axis_index("core")
    pl.when(core == 0)(lambda: form(prior, raw_next))
    pl.when(core == 1)(lambda: form(prior_last, raw))


def add_kernel(parts, *outs):
    *outs, whole = outs
    whole[...] = summed_rows([parts[x, c] for x in range(4) for c in range(2)])
    place = lax.axis_index("y")
    for d, out in enumerate(outs):
        out[...] = whole[pl.ds(pl.multiple_of((place + d) % 4 * 16, 16), 16)]


def plane_prefix_kernel(zero_a, zero_b, zero_c, zero_d, one, out, zero):
    place = lax.axis_index("y")
    for d, part in enumerate((zero_a, zero_b, zero_c, zero_d)):
        zero[(place + 4 - d) % 4] = part[...]
    zeros, ones, late = [], [], None
    for lag in range(4):
        zeros.append(zero[lag] if lag == 0 else zeros[-1] + zero[lag])
        here, after = (summed_blocks([one[lag, x, c] for x in range(4)]) for c in range(2))
        if lag == 0:
            late, total = after, here + after
        else:
            ones.append(total + after)
            total = total + here + after
    ones.append(total)
    first = 0
    for i, parts in enumerate((zeros, ones, [late])):
        value = jnp.concatenate(parts, axis=0)
        exponent = exponent_of(value)
        value = encode(value, exponent)
        height = value.shape[0]
        for zl in range(4):
            out[zl, first : first + height] = value[:, zl * 128 : (zl + 1) * 128]
            out[zl, 144 + i * 8 : 152 + i * 8] = jnp.broadcast_to(exponent, (8, 128))
        first += height


def block_prefix_kernel(planes, local, total):
    def read(zl, i, first):
        exponent = planes[zl, 144 + i * 8 : 152 + i * 8]
        exponent = jnp.concatenate([exponent, exponent], axis=0)
        return decode(planes[zl, first : first + 16], exponent)

    zero, one = jnp.zeros((16, 128), F32), jnp.zeros((16, 128), F32)
    lates = [read(zl, 2, 128) for zl in range(4)]
    for zl in range(4):
        for lag in range(4):
            here_zero = zero + read(zl, 0, lag * 16)
            here_one = one + read(zl, 1, 64 + lag * 16)
            local[zl * 4 + lag, 0:16] = here_zero
            local[zl * 4 + lag, 16:32] = here_one + lates[zl + 1] if lag == 3 and zl < 3 else here_one
        zero, one = here_zero, here_one
    total[0:16], total[16:32], total[32:48] = zero, one, lates[0]


def sum_kernel(total, other, out):
    out[0:32] = total[0:32] + other[0:32]
    out[32:48] = total[32:48]


def finish_kernel(local, early, back, crossed, own, out):
    place = lax.axis_index("zh")

    def pick(chosen, ref, first, last):
        return jnp.where(chosen, ref[first:last], 0.0)

    earlier = pick(place == 1, early, 0, 32) + pick(place >= 2, crossed, 0, 32) + pick(place == 3, own, 0, 32)
    late = pick(place == 0, early, 32, 48) + pick(place == 1, back, 32, 48) + pick(place == 2, own, 32, 48)
    for i in range(16):
        out[i] = local[i] + earlier
    out[15, 16:32] = local[15, 16:32] + earlier[16:32] + late


def split_kernel(rows, zero, one):
    for zl in range(4):
        for y in range(4):
            here, there = slice(y * 16, (y + 1) * 16), slice(zl * 128, (zl + 1) * 128)
            zero[0, here, there] = rows[zl * 4 + y, 0:16]
            one[0, here, there] = rows[zl * 4 + y, 16:32]


def exchange(value, axes):
    return lax.all_to_all(value, axes, 0, 0, tiled=True)


def exchange_short(value, axes):
    return exchange(value.astype(F16), axes).astype(F32)


def body(prior_rows, raw_rows):
    prior, raw = prior_rows[0], raw_rows[0]
    device = np.arange(512).reshape(64, 4, 2)
    down = [(int(device[l + 1, x, 0]), int(device[l, x, 0])) for l in range(63) for x in range(4)]
    up = [(int(device[l, x, 1]), int(device[l + 1, x, 1])) for l in range(63) for x in range(4)]
    raw_next = lax.ppermute(raw, LAG + PAR, down)
    prior_last = lax.ppermute(prior, LAG + PAR, up)

    full = pltpu.VMEM((512, 2048), jnp.bfloat16)
    zero, prior, raw = pl.pallas_call(
        tile_zero_kernel,
        out_shape=(shape(4, 2, 8, 4224), full, full),
        in_specs=[pl.BlockSpec(memory_space=pltpu.HBM)] * 2,
        out_specs=(VMEM,) * 3,
        scratch_shapes=[pltpu.VMEM((512, 512), F32), pltpu.SemaphoreType.DMA((STEPS * 4,))],
        compiler_params=pltpu.CompilerParams(vmem_limit_bytes=8 * 2**20),
    )(far(prior), far(raw))
    zero = exchange_short(zero.reshape(8, 8, 4224), PAR).reshape(4, 2, 8, 4224)
    rows = call(add_kernel, (shape(16, 512),) * 4, zero, scratch=(shape(64, 512),))
    zero = [rows[0]]
    for d in range(1, 4):
        zero.append(lax.ppermute(rows[d], "y", [(i, (i + d) % 4) for i in range(4)]))

    one = call(tile_one_kernel, shape(4, 4, 2, 8, 1152), prior, raw_next, prior_last, raw)
    one = exchange_short(one.reshape(32, 8, 1152), ("y", "x", "core")).reshape(4, 4, 2, 8, 1152)

    planes = exchange_short(call(plane_prefix_kernel, shape(4, 168, 128), *zero, one, scratch=(shape(4, 16, 512),)), "zl")
    local, total = call(block_prefix_kernel, (shape(16, 32, 128), shape(48, 128)), planes)
    early = lax.ppermute(total, "zh", [(0, 1), (1, 0)])
    back = lax.ppermute(total, "zh", [(2, 1)])
    both = call(sum_kernel, shape(48, 128), total, early)
    crossed = lax.ppermute(both, "zh", [(1, 2), (0, 3)])
    own = lax.ppermute(total, "zh", [(2, 3), (3, 2)])
    rows = call(finish_kernel, shape(16, 32, 128), local, early, back, crossed, own)
    return tuple(call(split_kernel, (result(1, 64, 512), result(1, 64, 512)), exchange(rows, ("zl", "y"))))


def solution(mesh):
    chips = Mesh(mesh.devices.reshape(4, 4, 4, 4, 2), LAG + PAR)
    in_specs = (P(LAG, None, PAR), P(LAG, None, PAR))
    out_specs = (P(LAG, PAR, None), P(LAG, PAR, None))
    return jax.shard_map(body, mesh=chips, in_specs=in_specs, out_specs=out_specs, check_vma=False)
```

```python
import jax
import jax.numpy as jnp
import numpy as np
from jax import lax
from jax.experimental import pallas as pl
from jax.experimental.pallas import tpu as pltpu
from jax.sharding import Mesh, PartitionSpec as P


F32 = jnp.float32
F16 = jnp.float16
NT = (((1,), (1,)), ((), ()))
LAG = ("zh", "zl", "y")
PAR = ("x", "core")
VMEM = pl.BlockSpec(memory_space=pltpu.VMEM)
STEPS = 4


def near(value):
    return pltpu.with_memory_space_constraint(value, pltpu.VMEM)


def far(value):
    return pltpu.with_memory_space_constraint(value, pltpu.HBM)


def call(kernel, out_shape, *args, scratch=()):
    return pl.pallas_call(
        kernel,
        out_shape=out_shape,
        scratch_shapes=scratch,
        in_specs=[VMEM] * len(args),
        out_specs=jax.tree.map(lambda _: VMEM, out_shape),
        compiler_params=pltpu.CompilerParams(vmem_limit_bytes=6 * 2**20),
    )(*[near(arg) for arg in args])


def shape(*dims):
    return pltpu.VMEM(dims, F32)


def result(*dims):
    return jax.ShapeDtypeStruct(dims, F32)


def exponent_of(value):
    top = jnp.max(jnp.max(jnp.abs(value), axis=0, keepdims=True), axis=1, keepdims=True)
    return jnp.floor(jnp.log2(jnp.maximum(top, 1e-30)))


LEVEL = 3.3


def encode(value, exponent):
    size = jnp.abs(value) * jnp.exp2(7.0 - exponent)
    binade = jnp.floor(jnp.log2(jnp.maximum(size, 1.0)))
    place = LEVEL * (binade + size * jnp.exp2(-binade))
    whole = jnp.floor(place)
    code = jnp.exp2(whole - 14.0) * (1.0 + (place - whole))
    return jnp.where(value < 0, -code, code)


def decode(code, exponent):
    size = jnp.abs(code)
    whole = jnp.floor(jnp.log2(jnp.maximum(size, 2.0**-14)))
    place = (whole + 13.0 + size * jnp.exp2(-whole)) * (1.0 / LEVEL)
    binade = jnp.maximum(jnp.floor(place) - 1.0, 0.0)
    value = (place - binade) * jnp.exp2(binade + exponent - 7.0)
    return jnp.where(code < 0, -value, value)


def pack_rows(tile, out):
    exponent = exponent_of(tile)
    tail = jnp.broadcast_to(exponent, (8, 128))
    sent = tile * jnp.exp2(14.0 - exponent)
    for x in range(4):
        for c in range(2):
            first = x * 128 + c * 64
            groups = [sent[first + i * 8 : first + (i + 1) * 8] for i in range(8)]
            out[x, c] = jnp.concatenate(groups + [tail], axis=1)


def summed_rows(parts):
    groups = [None] * 8
    for part in parts:
        scale = jnp.exp2(part[:, 4096:] - 14.0)
        scale = jnp.concatenate([scale] * 4, axis=1)
        for i in range(8):
            group = part[:, i * 512 : (i + 1) * 512] * scale
            groups[i] = group if groups[i] is None else groups[i] + group
    return jnp.concatenate(groups, axis=0)


def pack_blocks(tile, out):
    exponent = exponent_of(tile)
    tail = jnp.broadcast_to(exponent, (8, 128))
    sent = tile * jnp.exp2(14.0 - exponent)
    for x in range(4):
        for c in range(2):
            for y in range(4):
                first = x * 128 + c * 64 + y * 16
                top, bottom = sent[first : first + 8], sent[first + 8 : first + 16]
                out[y, x, c] = jnp.concatenate([top, bottom, tail], axis=1)


def unpack(sent):
    scale = jnp.exp2(sent[:, 1024:] - 14.0)
    scale = jnp.concatenate([scale] * 4, axis=1)
    return sent[:, :512] * scale, sent[:, 512:1024] * scale


def summed_blocks(parts):
    top, bottom = unpack(parts[0])
    for part in parts[1:]:
        more_top, more_bottom = unpack(part)
        top, bottom = top + more_top, bottom + more_bottom
    return jnp.concatenate([top, bottom], axis=0)


def tile_zero_kernel(prior, raw, out, prior_near, raw_near, total, sems):
    width = 2048 // STEPS
    copies = []
    for step in range(STEPS):
        group = []
        for i in range(4):
            source, target = (prior, prior_near) if i < 2 else (raw, raw_near)
            piece = (pl.ds(i % 2 * 256, 256), pl.ds(step * width, width))
            group.append(pltpu.make_async_copy(source.at[piece], target.at[piece], sems.at[step * 4 + i]))
        copies.append(group)
    for group in copies:
        for copy in group:
            copy.start()
    for step, group in enumerate(copies):
        for copy in group:
            copy.wait()
        columns = slice(step * width, (step + 1) * width)
        part = lax.dot_general(prior_near[:, columns], raw_near[:, columns], NT, preferred_element_type=F32)
        if step == 0:
            total[...] = part
        else:
            total[...] += part
    pack_rows(total[...], out)


def tile_one_kernel(prior, raw_next, prior_last, raw, out):
    def form(left, right):
        pack_blocks(lax.dot_general(left[...], right[...], NT, preferred_element_type=F32), out)

    core = lax.axis_index("core")
    pl.when(core == 0)(lambda: form(prior, raw_next))
    pl.when(core == 1)(lambda: form(prior_last, raw))


def add_kernel(parts, *outs):
    *outs, whole = outs
    whole[...] = summed_rows([parts[x, c] for x in range(4) for c in range(2)])
    place = lax.axis_index("y")
    for d, out in enumerate(outs):
        out[...] = whole[pl.ds(pl.multiple_of((place ^ d) * 16, 16), 16)]


def plane_prefix_kernel(zero_a, zero_b, zero_c, zero_d, one, out, zero):
    place = lax.axis_index("y")
    for d, part in enumerate((zero_a, zero_b, zero_c, zero_d)):
        zero[place ^ d] = part[...]
    zeros, ones, late = [], [], None
    for lag in range(4):
        zeros.append(zero[lag] if lag == 0 else zeros[-1] + zero[lag])
        here, after = (summed_blocks([one[lag, x, c] for x in range(4)]) for c in range(2))
        if lag == 0:
            late, total = after, here + after
        else:
            ones.append(total + after)
            total = total + here + after
    ones.append(total)
    first = 0
    for i, parts in enumerate((zeros, ones, [late])):
        value = jnp.concatenate(parts, axis=0)
        exponent = exponent_of(value)
        value = encode(value, exponent)
        height = value.shape[0]
        for zl in range(4):
            out[zl, first : first + height] = value[:, zl * 128 : (zl + 1) * 128]
            out[zl, 144 + i * 8 : 152 + i * 8] = jnp.broadcast_to(exponent, (8, 128))
        first += height


def block_prefix_kernel(planes, local, total):
    def read(zl, i, first):
        exponent = planes[zl, 144 + i * 8 : 152 + i * 8]
        exponent = jnp.concatenate([exponent, exponent], axis=0)
        return decode(planes[zl, first : first + 16], exponent)

    zero, one = jnp.zeros((16, 128), F32), jnp.zeros((16, 128), F32)
    lates = [read(zl, 2, 128) for zl in range(4)]
    for zl in range(4):
        for lag in range(4):
            here_zero = zero + read(zl, 0, lag * 16)
            here_one = one + read(zl, 1, 64 + lag * 16)
            local[zl * 4 + lag, 0:16] = here_zero
            local[zl * 4 + lag, 16:32] = here_one + lates[zl + 1] if lag == 3 and zl < 3 else here_one
        zero, one = here_zero, here_one
    total[0:16], total[16:32], total[32:48] = zero, one, lates[0]


def sum_kernel(total, other, out):
    out[0:32] = total[0:32] + other[0:32]
    out[32:48] = total[32:48]


def finish_kernel(local, early, back, crossed, own, out):
    place = lax.axis_index("zh")

    def pick(chosen, ref, first, last):
        return jnp.where(chosen, ref[first:last], 0.0)

    earlier = pick(place == 1, early, 0, 32) + pick(place >= 2, crossed, 0, 32) + pick(place == 3, own, 0, 32)
    late = pick(place == 0, early, 32, 48) + pick(place == 1, back, 32, 48) + pick(place == 2, own, 32, 48)
    for i in range(16):
        out[i] = local[i] + earlier
    out[15, 16:32] = local[15, 16:32] + earlier[16:32] + late


def split_kernel(rows, zero, one):
    for zl in range(4):
        for y in range(4):
            here, there = slice(y * 16, (y + 1) * 16), slice(zl * 128, (zl + 1) * 128)
            zero[0, here, there] = rows[zl * 4 + y, 0:16]
            one[0, here, there] = rows[zl * 4 + y, 16:32]


def exchange(value, axes):
    return lax.all_to_all(value, axes, 0, 0, tiled=True)


def exchange_short(value, axes):
    return exchange(value.astype(F16), axes).astype(F32)


def body(prior_rows, raw_rows):
    prior, raw = prior_rows[0], raw_rows[0]
    device = np.arange(512).reshape(64, 4, 2)
    down = [(int(device[l + 1, x, 0]), int(device[l, x, 0])) for l in range(63) for x in range(4)]
    up = [(int(device[l, x, 1]), int(device[l + 1, x, 1])) for l in range(63) for x in range(4)]
    raw_next = lax.ppermute(raw, LAG + PAR, down)
    prior_last = lax.ppermute(prior, LAG + PAR, up)

    full = pltpu.VMEM((512, 2048), jnp.bfloat16)
    zero, prior, raw = pl.pallas_call(
        tile_zero_kernel,
        out_shape=(shape(4, 2, 8, 4224), full, full),
        in_specs=[pl.BlockSpec(memory_space=pltpu.HBM)] * 2,
        out_specs=(VMEM,) * 3,
        scratch_shapes=[pltpu.VMEM((512, 512), F32), pltpu.SemaphoreType.DMA((STEPS * 4,))],
        compiler_params=pltpu.CompilerParams(vmem_limit_bytes=8 * 2**20),
    )(far(prior), far(raw))
    zero = exchange_short(zero.reshape(8, 8, 4224), PAR).reshape(4, 2, 8, 4224)
    rows = call(add_kernel, (shape(16, 512),) * 4, zero, scratch=(shape(64, 512),))
    zero = [rows[0]]
    for d in range(1, 4):
        zero.append(lax.ppermute(rows[d], "y", [(i, i ^ d) for i in range(4)]))

    one = call(tile_one_kernel, shape(4, 4, 2, 8, 1152), prior, raw_next, prior_last, raw)
    one = exchange_short(one.reshape(32, 8, 1152), ("y", "x", "core")).reshape(4, 4, 2, 8, 1152)

    planes = exchange_short(call(plane_prefix_kernel, shape(4, 168, 128), *zero, one, scratch=(shape(4, 16, 512),)), "zl")
    local, total = call(block_prefix_kernel, (shape(16, 32, 128), shape(48, 128)), planes)
    early = lax.ppermute(total, "zh", [(0, 1), (1, 0)])
    back = lax.ppermute(total, "zh", [(2, 1)])
    both = call(sum_kernel, shape(48, 128), total, early)
    crossed = lax.ppermute(both, "zh", [(1, 2), (0, 3)])
    own = lax.ppermute(total, "zh", [(2, 3), (3, 2)])
    rows = call(finish_kernel, shape(16, 32, 128), local, early, back, crossed, own)
    return tuple(call(split_kernel, (result(1, 64, 512), result(1, 64, 512)), exchange(rows, ("zl", "y"))))


def solution(mesh):
    chips = Mesh(mesh.devices.reshape(4, 4, 4, 4, 2), LAG + PAR)
    in_specs = (P(LAG, None, PAR), P(LAG, None, PAR))
    out_specs = (P(LAG, PAR, None), P(LAG, PAR, None))
    return jax.shard_map(body, mesh=chips, in_specs=in_specs, out_specs=out_specs, check_vma=False)
```
